512 devices in a mesh: sec: 16 (over x, z_lo), blk: 32 (over y, z_hi, core).
Axes of the slice: x: 4, y: 4, z: 16 (z_hi: 4, z_lo: 4; z = z_hi * 4 + z_lo), core: 2. Of those that a mesh axis runs over, the one named last changes fastest.
Arguments:
- velocity: bfloat16 [64, 3, 1024, 512], P(None, None, ('sec', 'blk')), may hold values from -6 to 6
- geometry: float32 [9, 1024, 512], P(None, ('sec', 'blk')), may hold values from -4 to 4
- mass: float32 [1024, 512], P(('sec', 'blk')), may hold values from 0.5 to 2
- snapshots: bfloat16 [512, 3, 1024, 512], P(None, None, ('sec', 'blk')), may hold values from -6 to 6
- eigvecs: float32 [512, 256], P('blk'), may hold values from -0.25 to 0.25
- mode_order: int32 [256], replicated, may hold values from 0 to 255, each once
- elem_map: int32 [1024], P(('sec', 'blk')), may hold values from 0 to 1, as said below
Outputs:
- coefficients: float32 [64, 256], P('sec', 'blk')
The draws below stay inside these ranges and needn't reach their ends.
Inputs may be any that keep to these rules, and one draw needn't show every extreme that they name: `elem_map`: each aligned run of 2 entries (the elements of one device) holds each of 0 to 1 once. `mode_order`: A permutation of the modes.
All inputs are finite; a program needn't handle non-finite values.
Results may differ from the reference program's by a relative error of at most 0.0075.
Values sent between devices are 32-bit elements; how exact they have to be, the bound alone decides.
A program may use at most 64 MiB of HBM per device.

```python
import math
import jax
import jax.numpy as jnp
import numpy as np
from jax import lax

PTS = 512
MODES = 256
M = 512
E_DEV = 2
FIELDS = 64
ELEMS = 1024


def block_permutation(key):
    return jax.random.permutation(key, E_DEV)


def draw_elem_map(key, part):
    groups = ELEMS // E_DEV
    keys = jax.random.split(jax.random.fold_in(key, 11), groups)
    perms = jax.vmap(block_permutation)(keys)
    return perms.reshape(ELEMS).astype(jnp.int32)


def levels(stream_key, extent, pieces, least, high):
    factor_of, own = 1.0, jax.random.fold_in(stream_key, 6)
    for dim, parts in pieces:
        steps = jnp.exp(jax.random.uniform(jax.random.fold_in(own, dim), (parts,), jnp.float32, least / len(pieces), high / len(pieces)))
        factor_of = factor_of * jnp.repeat(steps, extent[dim] // parts).reshape([-1 if axis == dim else 1 for axis in range(len(extent))])
    return factor_of


def gaussian(rng, dims, spread, most, cuts=(), held_as=jnp.bfloat16):
    values = spread * jax.random.normal(rng, dims, jnp.float32)
    if cuts:
        values = values * levels(rng, dims, cuts, -0.22, 0.18)
    return jnp.clip(values, -most, most).astype(held_as)


def setup_inputs(seed: int = 0) -> dict:
    streams_of = jax.random.split(jax.random.key(seed), 8)
    velocity = gaussian(streams_of[0], (FIELDS, 3, ELEMS, PTS), 1.0, 6.0, ((2, 512),))
    geometry = gaussian(streams_of[1], (9, ELEMS, PTS), 0.3, 4.0, ((1, 512),), jnp.float32)
    mass = jnp.clip(jnp.exp(math.log(2.0) - 1.3862944 * jax.random.uniform(streams_of[2], (ELEMS, PTS), jnp.float32) ** levels(streams_of[2], (ELEMS, PTS), ((0, 512),), -0.2, 0.2)), 0.5, 2.0)
    snapshots = gaussian(streams_of[3], (M, 3, ELEMS, PTS), 1.0, 6.0, ((2, 512),))
    eigvecs = gaussian(streams_of[4], (M, MODES), M ** -0.5, 0.25, ((0, 32),), jnp.float32)
    mode_order = jax.random.permutation(streams_of[5], MODES).astype(jnp.int32)
    elem_map = draw_elem_map(jax.random.fold_in(streams_of[7], 71), 0)
    return {"velocity": velocity, "geometry": geometry, "mass": mass, "snapshots": snapshots, "eigvecs": eigvecs, "mode_order": mode_order, "elem_map": elem_map}


GLL_NODES = np.array([-1.0, -0.8717401485096066, -0.5917001814331423, -0.2092992179024789, 0.2092992179024789, 0.5917001814331423, 0.8717401485096066, 1.0])
GLL_WEIGHTS = np.array([1.0 / 28.0, 0.2107042271435061, 0.3411226924835044, 0.4124587946587038, 0.4124587946587038, 0.3411226924835044, 0.2107042271435061, 1.0 / 28.0])

def legendre_seven(nodes):
    before = nodes * 0.0 + 1.0
    current = nodes * 1.0
    for order in range(1, 7):
        following = ((2.0 * order + 1.0) * nodes * current - order * before) / (order + 1.0)
        before = current
        current = following
    return current

def derivative_matrix():
    degree = 7
    values = legendre_seven(GLL_NODES)
    result = np.zeros((8, 8))
    for row_idx in range(8):
        for col_idx in range(8):
            if row_idx != col_idx:
                result[row_idx, col_idx] = values[row_idx] / (values[col_idx] * (GLL_NODES[row_idx] - GLL_NODES[col_idx]))
    result[0, 0] = -degree * (degree + 1) / 4.0
    result[7, 7] = degree * (degree + 1) / 4.0
    return result

def point_weights():
    cube = GLL_WEIGHTS[:, None, None] * GLL_WEIGHTS[None, :, None] * GLL_WEIGHTS[None, None, :]
    return cube.reshape(512)

def reference(velocity, geometry, mass, snapshots, eigvecs, mode_order, elem_map):
    table = jnp.asarray(derivative_matrix(), jnp.float32)
    weight_cube = jnp.asarray(point_weights(), jnp.float32)
    highest = lax.Precision.HIGHEST
    groups = ELEMS // E_DEV

    def step(carry, group):
        start = (group * E_DEV).astype(jnp.int32)
        velocity_block = lax.dynamic_slice_in_dim(velocity, start, E_DEV, 2)
        geometry_block = lax.dynamic_slice_in_dim(geometry, start, E_DEV, 1)
        mass_block = lax.dynamic_slice_in_dim(mass, start, E_DEV, 0)
        snapshot_block = lax.dynamic_slice_in_dim(snapshots, start, E_DEV, 2)
        map_block = lax.dynamic_slice_in_dim(elem_map, start, E_DEV, 0).astype(jnp.int32)
        cube = velocity_block.astype(jnp.float32).reshape(FIELDS, 3, E_DEV, 8, 8, 8)
        along_r = jnp.einsum('ai,scdijk->scdajk', table, cube, precision=highest).reshape(FIELDS, 3, E_DEV, PTS)
        along_s = jnp.einsum('aj,scdijk->scdiak', table, cube, precision=highest).reshape(FIELDS, 3, E_DEV, PTS)
        along_t = jnp.einsum('ak,scdijk->scdija', table, cube, precision=highest).reshape(FIELDS, 3, E_DEV, PTS)

        def gradient(component, coord):
            return geometry_block[coord] * along_r[:, component] + geometry_block[3 + coord] * along_s[:, component] + geometry_block[6 + coord] * along_t[:, component]
        vorticity = jnp.stack([gradient(2, 1) - gradient(1, 2), gradient(0, 2) - gradient(2, 0), gradient(1, 0) - gradient(0, 1)], axis=1)
        weighted = (mass_block * weight_cube * vorticity).astype(jnp.bfloat16)
        chosen = jnp.take(snapshot_block, map_block, axis=2)
        update = jnp.dot(weighted.reshape(FIELDS, 3 * E_DEV * PTS), chosen.reshape(M, 3 * E_DEV * PTS).T, preferred_element_type=jnp.float32)
        return (carry + update, None)
    init = jnp.zeros((FIELDS, M), jnp.float32)
    contracted, _ = lax.scan(step, init, jnp.arange(groups, dtype=jnp.int32))
    ordered = eigvecs[:, mode_order]
    return jnp.dot(contracted, ordered, precision=highest) * (0.25 / math.sqrt(ELEMS))
```

```python
import functools
import math

import jax
import jax.numpy as jnp
import numpy as np
from jax import lax
from jax.experimental import pallas as pl
from jax.experimental.pallas import tpu as pltpu
from jax.sharding import PartitionSpec as P

GLL_NODES = np.array(
    [
        -1.0,
        -0.8717401485096066,
        -0.5917001814331423,
        -0.2092992179024789,
        0.2092992179024789,
        0.5917001814331423,
        0.8717401485096066,
        1.0,
    ]
)
GLL_WEIGHTS = np.array(
    [
        1.0 / 28.0,
        0.2107042271435061,
        0.3411226924835044,
        0.4124587946587038,
        0.4124587946587038,
        0.3411226924835044,
        0.2107042271435061,
        1.0 / 28.0,
    ]
)


def legendre_seven(nodes):
    before = nodes * 0.0 + 1.0
    current = nodes * 1.0
    for order in range(1, 7):
        following = ((2.0 * order + 1.0) * nodes * current - order * before) / (order + 1.0)
        before = current
        current = following
    return current


def derivative_matrix():
    degree = 7
    values = legendre_seven(GLL_NODES)
    result = np.zeros((8, 8))
    for row_idx in range(8):
        for col_idx in range(8):
            if row_idx != col_idx:
                result[row_idx, col_idx] = values[row_idx] / (
                    values[col_idx] * (GLL_NODES[row_idx] - GLL_NODES[col_idx])
                )
    result[0, 0] = -degree * (degree + 1) / 4.0
    result[7, 7] = degree * (degree + 1) / 4.0
    return result.astype(np.float32)


def point_weights():
    cube = GLL_WEIGHTS[:, None, None] * GLL_WEIGHTS[None, :, None] * GLL_WEIGHTS[None, None, :]
    return cube.reshape(512).astype(np.float32)


MESH_IDS = pl.DeviceIdType.MESH
F32 = jnp.float32
BF16 = jnp.bfloat16


def vorticity_weighted(velocity, geometry, mass):
    fields, components, elements, points = velocity.shape
    highest = lax.Precision.HIGHEST
    table = jnp.asarray(derivative_matrix())
    cube = velocity.astype(jnp.float32).reshape(fields, components, elements, 8, 8, 8)
    along_r = jnp.einsum("ai,scdijk->scdajk", table, cube, precision=highest).reshape(
        fields, components, elements, points
    )
    along_s = jnp.einsum("aj,scdijk->scdiak", table, cube, precision=highest).reshape(
        fields, components, elements, points
    )
    along_t = jnp.einsum("ak,scdijk->scdija", table, cube, precision=highest).reshape(
        fields, components, elements, points
    )

    def gradient(component, coord):
        return (
            geometry[coord] * along_r[:, component]
            + geometry[3 + coord] * along_s[:, component]
            + geometry[6 + coord] * along_t[:, component]
        )

    vorticity = jnp.stack(
        [
            gradient(2, 1) - gradient(1, 2),
            gradient(0, 2) - gradient(2, 0),
            gradient(1, 0) - gradient(0, 1),
        ],
        axis=1,
    )
    return (mass * jnp.asarray(point_weights()) * vorticity).astype(jnp.bfloat16)


def split_dot(a, b):
    a_hi = a.astype(BF16)
    a_lo = (a - a_hi.astype(F32)).astype(BF16)
    b_hi = b.astype(BF16)
    b_lo = (b - b_hi.astype(F32)).astype(BF16)
    out = jnp.dot(a_hi, b_hi, preferred_element_type=F32)
    out = out + jnp.dot(a_hi, b_lo, preferred_element_type=F32)
    return out + jnp.dot(a_lo, b_hi, preferred_element_type=F32)


def comm_kernel(nsec, nblk, factor, cin_ref, eb_ref, out_ref,
                r1, eg, s2, r2, ss1, rs1, ssg, rsg, ss2, rs2, lsem):
    s = lax.axis_index("sec")
    b = lax.axis_index("blk")

    barrier = pltpu.get_barrier_semaphore()

    def greet_sec(d, c):
        peer = lax.rem(s + d, nsec)
        pl.semaphore_signal(barrier, 1, device_id=(peer, b), device_id_type=MESH_IDS)
        return c

    def greet_blk(d, c):
        peer = lax.rem(b + d, nblk)
        pl.semaphore_signal(barrier, 1, device_id=(s, peer), device_id_type=MESH_IDS)
        return c

    lax.fori_loop(1, nsec, greet_sec, 0)
    lax.fori_loop(1, nblk, greet_blk, 0)
    pl.semaphore_wait(barrier, (nsec - 1) + (nblk - 1))

    def gather_copy(j):
        return pltpu.make_async_remote_copy(
            eb_ref, eg.at[b], ssg.at[j], rsg.at[b],
            device_id=(s, j), device_id_type=MESH_IDS)

    def gather_recv(j):
        return pltpu.make_async_remote_copy(
            eb_ref, eg.at[j], ssg.at[j], rsg.at[j],
            device_id=(s, j), device_id_type=MESH_IDS)

    def sec_copy(j):
        return pltpu.make_async_remote_copy(
            cin_ref.at[j], r1.at[s], ss1.at[j], rs1.at[s],
            device_id=(j, b), device_id_type=MESH_IDS)

    def sec_recv(j):
        return pltpu.make_async_remote_copy(
            cin_ref.at[j], r1.at[j], ss1.at[j], rs1.at[j],
            device_id=(j, b), device_id_type=MESH_IDS)

    def blk_copy(j):
        return pltpu.make_async_remote_copy(
            s2.at[j], r2.at[b], ss2.at[j], rs2.at[b],
            device_id=(s, j), device_id_type=MESH_IDS)

    def blk_recv(j):
        return pltpu.make_async_remote_copy(
            s2.at[j], r2.at[j], ss2.at[j], rs2.at[j],
            device_id=(s, j), device_id_type=MESH_IDS)

    own_eb = pltpu.make_async_copy(eb_ref, eg.at[b], lsem.at[0])
    own_eb.start()

    def start_gather(d, c):
        gather_copy(lax.rem(b + d, nblk)).start()
        return c

    def start_sec(d, c):
        sec_copy(lax.rem(s + d, nsec)).start()
        return c

    lax.fori_loop(1, nsec, start_sec, 0)
    lax.fori_loop(1, nblk, start_gather, 0)

    def sum_sec(d, acc):
        j = lax.rem(s + d, nsec)
        sec_recv(j).wait_recv()
        return acc + r1[j]

    cb = lax.fori_loop(1, nsec, sum_sec, cin_ref[s])

    def wait_gather(d, c):
        gather_recv(lax.rem(b + d, nblk)).wait_recv()
        return c

    lax.fori_loop(1, nblk, wait_gather, 0)
    own_eb.wait()

    rows, modes = eb_ref.shape
    ordered = eg[...].reshape(nblk * rows, modes)
    q = split_dot(cb, ordered)
    width = 128
    per_window = width // (modes // nblk)
    step = modes // nblk
    for j in range(nblk):
        window = q[:, (j // per_window) * width:(j // per_window + 1) * width]
        shift = (width - step * (j % per_window)) % width
        s2[j] = pltpu.roll(window, shift, 1) if shift else window

    def start_blk(d, c):
        blk_copy(lax.rem(b + d, nblk)).start()
        return c

    lax.fori_loop(1, nblk, start_blk, 0)

    def wait_sends_sec(d, c):
        sec_copy(lax.rem(s + d, nsec)).wait_send()
        return c

    def wait_sends_gather(d, c):
        gather_copy(lax.rem(b + d, nblk)).wait_send()
        return c

    lax.fori_loop(1, nsec, wait_sends_sec, 0)
    lax.fori_loop(1, nblk, wait_sends_gather, 0)

    def sum_blk(d, acc):
        j = lax.rem(b + d, nblk)
        blk_recv(j).wait_recv()
        return acc + r2[j]

    total = lax.fori_loop(1, nblk, sum_blk, s2[b])
    out_ref[...] = total * factor

    def wait_sends_blk(d, c):
        blk_copy(lax.rem(b + d, nblk)).wait_send()
        return c

    lax.fori_loop(1, nblk, wait_sends_blk, 0)


def shards(velocity, geometry, mass, snapshots, eigvecs, mode_order, elem_map):
    nsec = lax.axis_size("sec")
    nblk = lax.axis_size("blk")
    weighted = vorticity_weighted(velocity, geometry, mass)
    fields, components, elements, points = weighted.shape
    slot_index = lax.broadcasted_iota(jnp.int32, (elements, elements), 0)
    onehot = (slot_index == elem_map[None, :]).astype(jnp.bfloat16)
    stored = jnp.einsum(
        "fe,scep->scfp", onehot, weighted, preferred_element_type=jnp.float32
    ).astype(jnp.bfloat16)
    local = lax.dot_general(
        stored, snapshots, (((1, 2, 3), (1, 2, 3)), ((), ())),
        preferred_element_type=F32)
    m_count = local.shape[1]
    per_sec = fields // nsec
    pad = (-per_sec) % 8
    cin = jnp.pad(local.reshape(nsec, per_sec, m_count), ((0, 0), (0, pad), (0, 0)))
    eb = jnp.take(eigvecs, mode_order, axis=1)
    rows, modes = eb.shape
    factor = 0.25 / math.sqrt(elements * nsec * nblk)
    kernel = functools.partial(comm_kernel, nsec, nblk, factor)
    out = pl.pallas_call(
        kernel,
        out_shape=jax.ShapeDtypeStruct((per_sec + pad, 128), F32),
        in_specs=[pl.BlockSpec(memory_space=pltpu.VMEM)] * 2,
        out_specs=pl.BlockSpec(memory_space=pltpu.VMEM),
        scratch_shapes=[
            pltpu.VMEM((nsec, per_sec + pad, m_count), F32),
            pltpu.VMEM((nblk, rows, modes), F32),
            pltpu.VMEM((nblk, per_sec + pad, 128), F32),
            pltpu.VMEM((nblk, per_sec + pad, 128), F32),
            pltpu.SemaphoreType.DMA((nsec,)),
            pltpu.SemaphoreType.DMA((nsec,)),
            pltpu.SemaphoreType.DMA((nblk,)),
            pltpu.SemaphoreType.DMA((nblk,)),
            pltpu.SemaphoreType.DMA((nblk,)),
            pltpu.SemaphoreType.DMA((nblk,)),
            pltpu.SemaphoreType.DMA((1,)),
        ],
        compiler_params=pltpu.CompilerParams(collective_id=0, has_side_effects=True),
    )(cin, eb)
    return out[:per_sec, : modes // nblk]


def solution(mesh):
    placed = (
        P(None, None, ("sec", "blk"), None),
        P(None, ("sec", "blk"), None),
        P(("sec", "blk"), None),
        P(None, None, ("sec", "blk"), None),
        P("blk", None),
        P(),
        P(("sec", "blk")),
    )
    return jax.shard_map(
        shards, mesh=mesh, in_specs=placed, out_specs=P("sec", "blk"), check_vma=False
    )
```

```python
import functools
import math

import jax
import jax.numpy as jnp
import numpy as np
from jax import lax
from jax.experimental import pallas as pl
from jax.experimental.pallas import tpu as pltpu
from jax.sharding import PartitionSpec as P

GLL_NODES = np.array(
    [
        -1.0,
        -0.8717401485096066,
        -0.5917001814331423,
        -0.2092992179024789,
        0.2092992179024789,
        0.5917001814331423,
        0.8717401485096066,
        1.0,
    ]
)
GLL_WEIGHTS = np.array(
    [
        1.0 / 28.0,
        0.2107042271435061,
        0.3411226924835044,
        0.4124587946587038,
        0.4124587946587038,
        0.3411226924835044,
        0.2107042271435061,
        1.0 / 28.0,
    ]
)


def legendre_seven(nodes):
    before = nodes * 0.0 + 1.0
    current = nodes * 1.0
    for order in range(1, 7):
        following = ((2.0 * order + 1.0) * nodes * current - order * before) / (order + 1.0)
        before = current
        current = following
    return current


def derivative_matrix():
    degree = 7
    values = legendre_seven(GLL_NODES)
    result = np.zeros((8, 8))
    for row_idx in range(8):
        for col_idx in range(8):
            if row_idx != col_idx:
                result[row_idx, col_idx] = values[row_idx] / (
                    values[col_idx] * (GLL_NODES[row_idx] - GLL_NODES[col_idx])
                )
    result[0, 0] = -degree * (degree + 1) / 4.0
    result[7, 7] = degree * (degree + 1) / 4.0
    return result.astype(np.float32)


def point_weights():
    cube = GLL_WEIGHTS[:, None, None] * GLL_WEIGHTS[None, :, None] * GLL_WEIGHTS[None, None, :]
    return cube.reshape(512).astype(np.float32)


MESH_IDS = pl.DeviceIdType.MESH
F32 = jnp.float32
BF16 = jnp.bfloat16


def vorticity_weighted(velocity, geometry, mass):
    fields, components, elements, points = velocity.shape
    highest = lax.Precision.HIGHEST
    table = jnp.asarray(derivative_matrix())
    cube = velocity.astype(jnp.float32).reshape(fields, components, elements, 8, 8, 8)
    along_r = jnp.einsum("ai,scdijk->scdajk", table, cube, precision=highest).reshape(
        fields, components, elements, points
    )
    along_s = jnp.einsum("aj,scdijk->scdiak", table, cube, precision=highest).reshape(
        fields, components, elements, points
    )
    along_t = jnp.einsum("ak,scdijk->scdija", table, cube, precision=highest).reshape(
        fields, components, elements, points
    )

    def gradient(component, coord):
        return (
            geometry[coord] * along_r[:, component]
            + geometry[3 + coord] * along_s[:, component]
            + geometry[6 + coord] * along_t[:, component]
        )

    vorticity = jnp.stack(
        [
            gradient(2, 1) - gradient(1, 2),
            gradient(0, 2) - gradient(2, 0),
            gradient(1, 0) - gradient(0, 1),
        ],
        axis=1,
    )
    return (mass * jnp.asarray(point_weights()) * vorticity).astype(jnp.bfloat16)


def split_dot(a, b):
    a_hi = a.astype(BF16)
    a_lo = (a - a_hi.astype(F32)).astype(BF16)
    b_hi = b.astype(BF16)
    b_lo = (b - b_hi.astype(F32)).astype(BF16)
    out = jnp.dot(a_hi, b_hi, preferred_element_type=F32)
    out = out + jnp.dot(a_hi, b_lo, preferred_element_type=F32)
    return out + jnp.dot(a_lo, b_hi, preferred_element_type=F32)


def comm_kernel(nsec, nblk, factor, cin_ref, eb_ref, out_ref,
                r1, s2, r2, s3, r3, ss1, rs1, ss2, rs2, ss3, rs3):
    s = lax.axis_index("sec")
    b = lax.axis_index("blk")

    barrier = pltpu.get_barrier_semaphore()

    def greet_sec(d, c):
        peer = lax.rem(s + d, nsec)
        pl.semaphore_signal(barrier, 1, device_id=(peer, b), device_id_type=MESH_IDS)
        return c

    def greet_blk(d, c):
        peer = lax.rem(b + d, nblk)
        pl.semaphore_signal(barrier, 1, device_id=(s, peer), device_id_type=MESH_IDS)
        return c

    lax.fori_loop(1, nsec, greet_sec, 0)
    lax.fori_loop(1, nblk, greet_blk, 0)
    pl.semaphore_wait(barrier, (nsec - 1) + (nblk - 1))

    def sec_copy(j, dst):
        return pltpu.make_async_remote_copy(
            cin_ref.at[j], r1.at[dst], ss1.at[j], rs1.at[dst],
            device_id=(j, b), device_id_type=MESH_IDS)

    def blk_copy(src, dst_slot, ssem, rsem, j, slot):
        return pltpu.make_async_remote_copy(
            src.at[j], dst_slot.at[slot], ssem.at[j], rsem.at[slot],
            device_id=(s, j), device_id_type=MESH_IDS)

    def over_sec(fn):
        def body(d, c):
            fn(lax.rem(s + d, nsec))
            return c
        lax.fori_loop(1, nsec, body, 0)

    def over_blk(fn):
        def body(d, c):
            fn(lax.rem(b + d, nblk))
            return c
        lax.fori_loop(1, nblk, body, 0)

    def reduce_sec(acc):
        def body(d, a):
            j = lax.rem(s + d, nsec)
            sec_copy(j, j).wait_recv()
            return a + r1[j]
        return lax.fori_loop(1, nsec, body, acc)

    def reduce_blk(send, recv, ssem, rsem):
        def body(d, a):
            j = lax.rem(b + d, nblk)
            blk_copy(send, recv, ssem, rsem, j, j).wait_recv()
            return a + recv[j]
        return lax.fori_loop(1, nblk, body, send[b])

    def pack(send, values, step):
        width = 128
        per_window = width // step
        for j in range(nblk):
            window = values[:, (j // per_window) * width:(j // per_window + 1) * width]
            shift = (width - step * (j % per_window)) % width
            send[j] = pltpu.roll(window, shift, 1) if shift else window

    over_sec(lambda j: sec_copy(j, s).start())
    cb = reduce_sec(cin_ref[s])

    modes = eb_ref.shape[1]
    rows = cb.shape[1] // nblk
    pack(s2, cb, rows)
    over_blk(lambda j: blk_copy(s2, r2, ss2, rs2, j, b).start())
    cf = reduce_blk(s2, r2, ss2, rs2)
    lane = lax.broadcasted_iota(jnp.int32, cf.shape, 1)
    cf = jnp.where(lane < rows, cf, 0.0)
    q = split_dot(cf, eb_ref[...])

    pack(s3, q, modes // nblk)
    over_blk(lambda j: blk_copy(s3, r3, ss3, rs3, j, b).start())
    over_sec(lambda j: sec_copy(j, s).wait_send())
    over_blk(lambda j: blk_copy(s2, r2, ss2, rs2, j, b).wait_send())
    total = reduce_blk(s3, r3, ss3, rs3)
    out_ref[...] = total * factor
    over_blk(lambda j: blk_copy(s3, r3, ss3, rs3, j, b).wait_send())


def shards(velocity, geometry, mass, snapshots, eigvecs, mode_order, elem_map):
    nsec = lax.axis_size("sec")
    nblk = lax.axis_size("blk")
    weighted = vorticity_weighted(velocity, geometry, mass)
    fields, components, elements, points = weighted.shape
    slot_index = lax.broadcasted_iota(jnp.int32, (elements, elements), 0)
    onehot = (slot_index == elem_map[None, :]).astype(jnp.bfloat16)
    stored = jnp.einsum(
        "fe,scep->scfp", onehot, weighted, preferred_element_type=jnp.float32
    ).astype(jnp.bfloat16)
    local = lax.dot_general(
        stored, snapshots, (((1, 2, 3), (1, 2, 3)), ((), ())),
        preferred_element_type=F32)
    m_count = local.shape[1]
    per_sec = fields // nsec
    pad = (-per_sec) % 8
    cin = jnp.pad(local.reshape(nsec, per_sec, m_count), ((0, 0), (0, pad), (0, 0)))
    eb = jnp.take(eigvecs, mode_order, axis=1)
    rows, modes = eb.shape
    eb_pad = jnp.pad(eb, ((0, 128 - rows), (0, 0)))
    factor = 0.25 / math.sqrt(elements * nsec * nblk)
    kernel = functools.partial(comm_kernel, nsec, nblk, factor)
    tile = (nblk, per_sec + pad, 128)
    out = pl.pallas_call(
        kernel,
        out_shape=jax.ShapeDtypeStruct((per_sec + pad, 128), F32),
        in_specs=[pl.BlockSpec(memory_space=pltpu.VMEM)] * 2,
        out_specs=pl.BlockSpec(memory_space=pltpu.VMEM),
        scratch_shapes=[
            pltpu.VMEM((nsec, per_sec + pad, m_count), F32),
            pltpu.VMEM(tile, F32),
            pltpu.VMEM(tile, F32),
            pltpu.VMEM(tile, F32),
            pltpu.VMEM(tile, F32),
            pltpu.SemaphoreType.DMA((nsec,)),
            pltpu.SemaphoreType.DMA((nsec,)),
            pltpu.SemaphoreType.DMA((nblk,)),
            pltpu.SemaphoreType.DMA((nblk,)),
            pltpu.SemaphoreType.DMA((nblk,)),
            pltpu.SemaphoreType.DMA((nblk,)),
        ],
        compiler_params=pltpu.CompilerParams(collective_id=0, has_side_effects=True),
    )(cin, eb_pad)
    return out[:per_sec, : modes // nblk]


def solution(mesh):
    placed = (
        P(None, None, ("sec", "blk"), None),
        P(None, ("sec", "blk"), None),
        P(("sec", "blk"), None),
        P(None, None, ("sec", "blk"), None),
        P("blk", None),
        P(),
        P(("sec", "blk")),
    )
    return jax.shard_map(
        shards, mesh=mesh, in_specs=placed, out_specs=P("sec", "blk"), check_vma=False
    )
```

```python
import functools
import math

import jax
import jax.numpy as jnp
import numpy as np
from jax import lax
from jax.experimental import pallas as pl
from jax.experimental.pallas import tpu as pltpu
from jax.sharding import PartitionSpec as P

GLL_NODES = np.array(
    [
        -1.0,
        -0.8717401485096066,
        -0.5917001814331423,
        -0.2092992179024789,
        0.2092992179024789,
        0.5917001814331423,
        0.8717401485096066,
        1.0,
    ]
)
GLL_WEIGHTS = np.array(
    [
        1.0 / 28.0,
        0.2107042271435061,
        0.3411226924835044,
        0.4124587946587038,
        0.4124587946587038,
        0.3411226924835044,
        0.2107042271435061,
        1.0 / 28.0,
    ]
)


def legendre_seven(nodes):
    before = nodes * 0.0 + 1.0
    current = nodes * 1.0
    for order in range(1, 7):
        following = ((2.0 * order + 1.0) * nodes * current - order * before) / (order + 1.0)
        before = current
        current = following
    return current


def derivative_matrix():
    degree = 7
    values = legendre_seven(GLL_NODES)
    result = np.zeros((8, 8))
    for row_idx in range(8):
        for col_idx in range(8):
            if row_idx != col_idx:
                result[row_idx, col_idx] = values[row_idx] / (
                    values[col_idx] * (GLL_NODES[row_idx] - GLL_NODES[col_idx])
                )
    result[0, 0] = -degree * (degree + 1) / 4.0
    result[7, 7] = degree * (degree + 1) / 4.0
    return result.astype(np.float32)


def point_weights():
    cube = GLL_WEIGHTS[:, None, None] * GLL_WEIGHTS[None, :, None] * GLL_WEIGHTS[None, None, :]
    return cube.reshape(512).astype(np.float32)


MESH_IDS = pl.DeviceIdType.MESH
F32 = jnp.float32
BF16 = jnp.bfloat16


def kron_matrices():
    dt = derivative_matrix().astype(np.float64).T
    eye8 = np.eye(8)
    along_r = np.kron(dt, np.eye(64))
    along_s = np.kron(eye8, np.kron(dt, eye8))
    along_t = np.kron(np.eye(64), dt)
    full = np.concatenate([along_r, along_s, along_t], axis=1).astype(np.float32)
    upper = jnp.asarray(full).astype(BF16)
    lower = (jnp.asarray(full) - upper.astype(F32)).astype(BF16)
    return upper, lower


def split_dot(a, b):
    a_hi = a.astype(BF16)
    a_lo = (a - a_hi.astype(F32)).astype(BF16)
    b_hi = b.astype(BF16)
    b_lo = (b - b_hi.astype(F32)).astype(BF16)
    out = jnp.dot(a_hi, b_hi, preferred_element_type=F32)
    out = out + jnp.dot(a_hi, b_lo, preferred_element_type=F32)
    return out + jnp.dot(a_lo, b_hi, preferred_element_type=F32)


def exact_select(a, onehot):
    hi = a.astype(BF16)
    rest = a - hi.astype(F32)
    mid = rest.astype(BF16)
    lo = (rest - mid.astype(F32)).astype(BF16)
    out = jnp.dot(hi, onehot, preferred_element_type=F32)
    out = out + jnp.dot(mid, onehot, preferred_element_type=F32)
    return out + jnp.dot(lo, onehot, preferred_element_type=F32)


def comm_kernel(nsec, nblk, factor, v_ref, mhi_ref, mlo_ref, geo_ref, mw_ref, snap_ref,
                em_ref, e_ref, sel_ref, out_ref,
                cin, r1, s2, r2, s3, r3, deriv, ss1, rs1, ss2, rs2, ss3, rs3):
    s = lax.axis_index("sec")
    b = lax.axis_index("blk")

    barrier = pltpu.get_barrier_semaphore()

    def greet_sec(d, c):
        peer = lax.rem(s + d, nsec)
        pl.semaphore_signal(barrier, 1, device_id=(peer, b), device_id_type=MESH_IDS)
        return c

    def greet_blk(d, c):
        peer = lax.rem(b + d, nblk)
        pl.semaphore_signal(barrier, 1, device_id=(s, peer), device_id_type=MESH_IDS)
        return c

    lax.fori_loop(1, nsec, greet_sec, 0)
    lax.fori_loop(1, nblk, greet_blk, 0)

    rows_v, pts = v_ref.shape
    comps = 3
    elems = mw_ref.shape[0]
    fields = rows_v // (comps * elems)
    v = v_ref[...]
    deriv[...] = (jnp.dot(v, mhi_ref[...], preferred_element_type=F32)
                  + jnp.dot(v, mlo_ref[...], preferred_element_type=F32))

    def along(a, c, e):
        row = (c * elems + e) * fields
        return deriv[row:row + fields, a * pts:(a + 1) * pts]

    weighted = []
    for e in range(elems):
        def geo(k):
            return geo_ref[k * elems + e:k * elems + e + 1, :]

        def gradient(c, coord):
            return (geo(coord) * along(0, c, e) + geo(3 + coord) * along(1, c, e)
                    + geo(6 + coord) * along(2, c, e))

        scale = mw_ref[e:e + 1, :]
        vort = [gradient(2, 1) - gradient(1, 2), gradient(0, 2) - gradient(2, 0),
                gradient(1, 0) - gradient(0, 1)]
        weighted.append([(scale * x).astype(BF16) for x in vort])

    local = jnp.zeros((fields, snap_ref.shape[1]), F32)
    for c in range(comps):
        for j in range(elems):
            stored = jnp.zeros_like(weighted[0][c])
            for e in range(elems):
                stored = jnp.where(em_ref[e] == j, weighted[e][c], stored)
            local = local + lax.dot_general(
                stored, snap_ref[c * elems + j], (((1,), (1,)), ((), ())),
                preferred_element_type=F32)

    per_sec = fields // nsec
    cin[...] = jnp.zeros(cin.shape, F32)
    for j in range(nsec):
        cin[j, 0:per_sec, :] = local[j * per_sec:(j + 1) * per_sec, :]

    eb = exact_select(e_ref[...], sel_ref[...])

    pl.semaphore_wait(barrier, (nsec - 1) + (nblk - 1))

    def sec_copy(j, dst):
        return pltpu.make_async_remote_copy(
            cin.at[j], r1.at[dst], ss1.at[j], rs1.at[dst],
            device_id=(j, b), device_id_type=MESH_IDS)

    def blk_copy(src, dst_slot, ssem, rsem, j, slot):
        return pltpu.make_async_remote_copy(
            src.at[j], dst_slot.at[slot], ssem.at[j], rsem.at[slot],
            device_id=(s, j), device_id_type=MESH_IDS)

    def over_sec(fn):
        def body(d, c):
            fn(lax.rem(s + d, nsec))
            return c
        lax.fori_loop(1, nsec, body, 0)

    def over_blk(fn):
        def body(d, c):
            fn(lax.rem(b + d, nblk))
            return c
        lax.fori_loop(1, nblk, body, 0)

    def reduce_sec(acc):
        def body(d, a):
            j = lax.rem(s + d, nsec)
            sec_copy(j, j).wait_recv()
            return a + r1[j]
        return lax.fori_loop(1, nsec, body, acc)

    def reduce_blk(send, recv, ssem, rsem):
        def body(d, a):
            j = lax.rem(b + d, nblk)
            blk_copy(send, recv, ssem, rsem, j, j).wait_recv()
            return a + recv[j]
        return lax.fori_loop(1, nblk, body, send[b])

    def pack(send, values, step):
        width = 128
        per_window = width // step
        for j in range(nblk):
            window = values[:, (j // per_window) * width:(j // per_window + 1) * width]
            shift = (width - step * (j % per_window)) % width
            send[j] = pltpu.roll(window, shift, 1) if shift else window

    over_sec(lambda j: sec_copy(j, s).start())
    cb = reduce_sec(cin[s])

    modes = e_ref.shape[1]
    rows = cb.shape[1] // nblk
    pack(s2, cb, rows)
    over_blk(lambda j: blk_copy(s2, r2, ss2, rs2, j, b).start())
    cf = reduce_blk(s2, r2, ss2, rs2)
    cf = cf[:, 0:rows]
    q = split_dot(cf, eb)

    pack(s3, q, modes // nblk)
    over_blk(lambda j: blk_copy(s3, r3, ss3, rs3, j, b).start())
    over_sec(lambda j: sec_copy(j, s).wait_send())
    over_blk(lambda j: blk_copy(s2, r2, ss2, rs2, j, b).wait_send())
    total = reduce_blk(s3, r3, ss3, rs3)
    out_ref[...] = total * factor
    over_blk(lambda j: blk_copy(s3, r3, ss3, rs3, j, b).wait_send())


def shards(velocity, geometry, mass, snapshots, eigvecs, mode_order, elem_map):
    nsec = lax.axis_size("sec")
    nblk = lax.axis_size("blk")
    fields, comps, elems, pts = velocity.shape
    m_count = snapshots.shape[0]
    v = jnp.transpose(velocity, (1, 2, 0, 3)).reshape(comps * elems * fields, pts)
    snap = jnp.transpose(snapshots, (1, 2, 0, 3)).reshape(comps * elems, m_count, pts)
    geo = geometry.reshape(9 * elems, pts)
    mw = mass * jnp.asarray(point_weights())
    modes = eigvecs.shape[1]
    sel = (lax.broadcasted_iota(jnp.int32, (modes, modes), 0) == mode_order[None, :]).astype(BF16)
    mhi, mlo = kron_matrices()
    per_sec = fields // nsec
    pad = (-per_sec) % 8
    factor = 0.25 / math.sqrt(elems * nsec * nblk)
    kernel = functools.partial(comm_kernel, nsec, nblk, factor)
    tile = (nblk, per_sec + pad, 128)
    vmem = pl.BlockSpec(memory_space=pltpu.VMEM)
    out = pl.pallas_call(
        kernel,
        out_shape=jax.ShapeDtypeStruct((per_sec + pad, 128), F32),
        in_specs=[vmem] * 6 + [pl.BlockSpec(memory_space=pltpu.SMEM)] + [vmem] * 2,
        out_specs=vmem,
        scratch_shapes=[
            pltpu.VMEM((nsec, per_sec + pad, m_count), F32),
            pltpu.VMEM((nsec, per_sec + pad, m_count), F32),
            pltpu.VMEM(tile, F32),
            pltpu.VMEM(tile, F32),
            pltpu.VMEM(tile, F32),
            pltpu.VMEM(tile, F32),
            pltpu.VMEM((comps * elems * fields, 3 * pts), F32),
            pltpu.SemaphoreType.DMA((nsec,)),
            pltpu.SemaphoreType.DMA((nsec,)),
            pltpu.SemaphoreType.DMA((nblk,)),
            pltpu.SemaphoreType.DMA((nblk,)),
            pltpu.SemaphoreType.DMA((nblk,)),
            pltpu.SemaphoreType.DMA((nblk,)),
        ],
        compiler_params=pltpu.CompilerParams(
            collective_id=0, has_side_effects=True, vmem_limit_bytes=48 * 1024 * 1024),
    )(v, mhi, mlo, geo, mw, snap, elem_map, eigvecs, sel)
    return out[:per_sec, : modes // nblk]


def solution(mesh):
    placed = (
        P(None, None, ("sec", "blk"), None),
        P(None, ("sec", "blk"), None),
        P(("sec", "blk"), None),
        P(None, None, ("sec", "blk"), None),
        P("blk", None),
        P(),
        P(("sec", "blk")),
    )
    return jax.shard_map(
        shards, mesh=mesh, in_specs=placed, out_specs=P("sec", "blk"), check_vma=False
    )
```

```python
import functools
import math

import jax
import jax.numpy as jnp
import numpy as np
from jax import lax
from jax.experimental import pallas as pl
from jax.experimental.pallas import tpu as pltpu
from jax.sharding import PartitionSpec as P

GLL_NODES = np.array(
    [
        -1.0,
        -0.8717401485096066,
        -0.5917001814331423,
        -0.2092992179024789,
        0.2092992179024789,
        0.5917001814331423,
        0.8717401485096066,
        1.0,
    ]
)
GLL_WEIGHTS = np.array(
    [
        1.0 / 28.0,
        0.2107042271435061,
        0.3411226924835044,
        0.4124587946587038,
        0.4124587946587038,
        0.3411226924835044,
        0.2107042271435061,
        1.0 / 28.0,
    ]
)


def legendre_seven(nodes):
    before = nodes * 0.0 + 1.0
    current = nodes * 1.0
    for order in range(1, 7):
        following = ((2.0 * order + 1.0) * nodes * current - order * before) / (order + 1.0)
        before = current
        current = following
    return current


def derivative_matrix():
    degree = 7
    values = legendre_seven(GLL_NODES)
    result = np.zeros((8, 8))
    for row_idx in range(8):
        for col_idx in range(8):
            if row_idx != col_idx:
                result[row_idx, col_idx] = values[row_idx] / (
                    values[col_idx] * (GLL_NODES[row_idx] - GLL_NODES[col_idx])
                )
    result[0, 0] = -degree * (degree + 1) / 4.0
    result[7, 7] = degree * (degree + 1) / 4.0
    return result.astype(np.float32)


def point_weights():
    cube = GLL_WEIGHTS[:, None, None] * GLL_WEIGHTS[None, :, None] * GLL_WEIGHTS[None, None, :]
    return cube.reshape(512).astype(np.float32)


MESH_IDS = pl.DeviceIdType.MESH
F32 = jnp.float32
BF16 = jnp.bfloat16


def kron_matrices():
    dt = derivative_matrix().astype(np.float64).T
    eye8 = np.eye(8)
    along_r = np.kron(dt, np.eye(64))
    along_s = np.kron(eye8, np.kron(dt, eye8))
    along_t = np.kron(np.eye(64), dt)
    full = np.concatenate([along_r, along_s, along_t], axis=1).astype(np.float32)
    upper = jnp.asarray(full).astype(BF16)
    lower = (jnp.asarray(full) - upper.astype(F32)).astype(BF16)
    return upper, lower


def split_dot(a, b):
    a_hi = a.astype(BF16)
    a_lo = (a - a_hi.astype(F32)).astype(BF16)
    b_hi = b.astype(BF16)
    b_lo = (b - b_hi.astype(F32)).astype(BF16)
    out = jnp.dot(a_hi, b_hi, preferred_element_type=F32)
    out = out + jnp.dot(a_hi, b_lo, preferred_element_type=F32)
    return out + jnp.dot(a_lo, b_hi, preferred_element_type=F32)


def exact_select(a, onehot):
    hi = a.astype(BF16)
    rest = a - hi.astype(F32)
    mid = rest.astype(BF16)
    lo = (rest - mid.astype(F32)).astype(BF16)
    out = jnp.dot(hi, onehot, preferred_element_type=F32)
    out = out + jnp.dot(mid, onehot, preferred_element_type=F32)
    return out + jnp.dot(lo, onehot, preferred_element_type=F32)


def comm_kernel(nsec, nblk, factor, v_ref, mhi_ref, mlo_ref, geo_ref, mw_ref, snap_ref,
                em_ref, e_ref, sel_ref, out_ref,
                cin, r1, eg, s2, r2, s3, r3, deriv, ss1, rs1, sse, rse, ss2, rs2, ss3, rs3):
    s = lax.axis_index("sec")
    b = lax.axis_index("blk")

    barrier = pltpu.get_barrier_semaphore()

    def greet_sec(d, c):
        peer = lax.rem(s + d, nsec)
        pl.semaphore_signal(barrier, 1, device_id=(peer, b), device_id_type=MESH_IDS)
        return c

    def greet_blk(d, c):
        peer = lax.rem(b + d, nblk)
        pl.semaphore_signal(barrier, 1, device_id=(s, peer), device_id_type=MESH_IDS)
        return c

    lax.fori_loop(1, nsec, greet_sec, 0)
    lax.fori_loop(1, nblk, greet_blk, 0)

    rows_v, pts = v_ref.shape
    comps = 3
    elems = mw_ref.shape[0]
    fields = rows_v // (comps * elems)
    v = v_ref[...]
    deriv[...] = (jnp.dot(v, mhi_ref[...], preferred_element_type=F32)
                  + jnp.dot(v, mlo_ref[...], preferred_element_type=F32))

    def along(a, c, e):
        row = (c * elems + e) * fields
        return deriv[row:row + fields, a * pts:(a + 1) * pts]

    weighted = []
    for e in range(elems):
        def geo(k):
            return geo_ref[k * elems + e:k * elems + e + 1, :]

        def gradient(c, coord):
            return (geo(coord) * along(0, c, e) + geo(3 + coord) * along(1, c, e)
                    + geo(6 + coord) * along(2, c, e))

        scale = mw_ref[e:e + 1, :]
        vort = [gradient(2, 1) - gradient(1, 2), gradient(0, 2) - gradient(2, 0),
                gradient(1, 0) - gradient(0, 1)]
        weighted.append([(scale * x).astype(BF16) for x in vort])

    local = jnp.zeros((fields, snap_ref.shape[1]), F32)
    for c in range(comps):
        for j in range(elems):
            stored = jnp.zeros_like(weighted[0][c])
            for e in range(elems):
                stored = jnp.where(em_ref[e] == j, weighted[e][c], stored)
            local = local + lax.dot_general(
                stored, snap_ref[c * elems + j], (((1,), (1,)), ((), ())),
                preferred_element_type=F32)

    per_sec = fields // nsec
    cin[...] = jnp.zeros(cin.shape, F32)
    for j in range(nsec):
        cin[j, 0:per_sec, :] = local[j * per_sec:(j + 1) * per_sec, :]

    pl.semaphore_wait(barrier, (nsec - 1) + (nblk - 1))

    zc = 4
    y = b // (2 * zc)
    z_hi = lax.rem(b // 2, zc)
    core = lax.rem(b, 2)
    g = y * 2 + core
    ng = nblk // zc

    def g_device(gp):
        return (gp // 2) * (2 * zc) + z_hi * 2 + lax.rem(gp, 2)

    def z_device(zp):
        return y * (2 * zc) + zp * 2 + core

    def sec_copy(j, dst):
        return pltpu.make_async_remote_copy(
            cin.at[j], r1.at[dst], ss1.at[j], rs1.at[dst],
            device_id=(j, b), device_id_type=MESH_IDS)

    def e_copy(zp, slot):
        return pltpu.make_async_remote_copy(
            e_ref, eg.at[slot], sse.at[zp], rse.at[slot],
            device_id=(s, z_device(zp)), device_id_type=MESH_IDS)

    def g_copy(gp, slot):
        return pltpu.make_async_remote_copy(
            s2.at[gp], r2.at[slot], ss2.at[gp], rs2.at[slot],
            device_id=(s, g_device(gp)), device_id_type=MESH_IDS)

    def blk_copy(j, slot):
        return pltpu.make_async_remote_copy(
            s3.at[j], r3.at[slot], ss3.at[j], rs3.at[slot],
            device_id=(s, j), device_id_type=MESH_IDS)

    def over(n, me, fn):
        def body(d, c):
            fn(lax.rem(me + d, n))
            return c
        lax.fori_loop(1, n, body, 0)

    def reduce(n, me, wait, recv, acc):
        def body(d, a):
            j = lax.rem(me + d, n)
            wait(j)
            return a + recv[j]
        return lax.fori_loop(1, n, body, acc)

    over(zc, z_hi, lambda zp: e_copy(zp, z_hi).start())
    over(nsec, s, lambda j: sec_copy(j, s).start())
    cb = reduce(nsec, s, lambda j: sec_copy(j, j).wait_recv(), r1, cin[s])

    modes = e_ref.shape[1]
    rows = cb.shape[1] // nblk
    width = 128
    lane_group = lax.broadcasted_iota(jnp.int32, (cb.shape[0], width), 1) // rows
    for gp in range(ng):
        packed = jnp.zeros((cb.shape[0], width), F32)
        for zp in range(zc):
            block = (gp // 2) * (2 * zc) + zp * 2 + gp % 2
            start = (block * rows) // width * width
            window = cb[:, start:start + width]
            shift = (rows * zp - (block * rows - start)) % width
            moved = pltpu.roll(window, shift, 1) if shift else window
            packed = jnp.where(lane_group == zp, moved, packed)
        s2[gp] = packed
    over(ng, g, lambda gp: g_copy(gp, g).start())

    eg[z_hi] = e_ref[...]
    over(zc, z_hi, lambda zp: e_copy(zp, zp).wait_recv())
    cp = reduce(ng, g, lambda gp: g_copy(gp, gp).wait_recv(), r2, s2[g])
    e_part = exact_select(eg[...].reshape(zc * e_ref.shape[0], modes), sel_ref[...])
    q = split_dot(cp[:, 0:zc * rows], e_part)

    step = modes // nblk
    per_window = width // step
    for j in range(nblk):
        window = q[:, (j // per_window) * width:(j // per_window + 1) * width]
        shift = (width - step * (j % per_window)) % width
        s3[j] = pltpu.roll(window, shift, 1) if shift else window
    over(nblk, b, lambda j: blk_copy(j, b).start())
    over(nsec, s, lambda j: sec_copy(j, s).wait_send())
    over(zc, z_hi, lambda zp: e_copy(zp, z_hi).wait_send())
    over(ng, g, lambda gp: g_copy(gp, g).wait_send())
    total = reduce(nblk, b, lambda j: blk_copy(j, j).wait_recv(), r3, s3[b])
    out_ref[...] = total * factor
    over(nblk, b, lambda j: blk_copy(j, b).wait_send())


def shards(velocity, geometry, mass, snapshots, eigvecs, mode_order, elem_map):
    nsec = lax.axis_size("sec")
    nblk = lax.axis_size("blk")
    fields, comps, elems, pts = velocity.shape
    m_count = snapshots.shape[0]
    v = jnp.transpose(velocity, (1, 2, 0, 3)).reshape(comps * elems * fields, pts)
    snap = jnp.transpose(snapshots, (1, 2, 0, 3)).reshape(comps * elems, m_count, pts)
    geo = geometry.reshape(9 * elems, pts)
    mw = mass * jnp.asarray(point_weights())
    modes = eigvecs.shape[1]
    sel = (lax.broadcasted_iota(jnp.int32, (modes, modes), 0) == mode_order[None, :]).astype(BF16)
    mhi, mlo = kron_matrices()
    per_sec = fields // nsec
    pad = (-per_sec) % 8
    factor = 0.25 / math.sqrt(elems * nsec * nblk)
    kernel = functools.partial(comm_kernel, nsec, nblk, factor)
    tile = (nblk, per_sec + pad, 128)
    vmem = pl.BlockSpec(memory_space=pltpu.VMEM)
    out = pl.pallas_call(
        kernel,
        out_shape=jax.ShapeDtypeStruct((per_sec + pad, 128), F32),
        in_specs=[vmem] * 6 + [pl.BlockSpec(memory_space=pltpu.SMEM)] + [vmem] * 2,
        out_specs=vmem,
        scratch_shapes=[
            pltpu.VMEM((nsec, per_sec + pad, m_count), F32),
            pltpu.VMEM((nsec, per_sec + pad, m_count), F32),
            pltpu.VMEM((4,) + eigvecs.shape, F32),
            pltpu.VMEM((nblk // 4, per_sec + pad, 128), F32),
            pltpu.VMEM((nblk // 4, per_sec + pad, 128), F32),
            pltpu.VMEM(tile, F32),
            pltpu.VMEM(tile, F32),
            pltpu.VMEM((comps * elems * fields, 3 * pts), F32),
            pltpu.SemaphoreType.DMA((nsec,)),
            pltpu.SemaphoreType.DMA((nsec,)),
            pltpu.SemaphoreType.DMA((4,)),
            pltpu.SemaphoreType.DMA((4,)),
            pltpu.SemaphoreType.DMA((nblk // 4,)),
            pltpu.SemaphoreType.DMA((nblk // 4,)),
            pltpu.SemaphoreType.DMA((nblk,)),
            pltpu.SemaphoreType.DMA((nblk,)),
        ],
        compiler_params=pltpu.CompilerParams(
            collective_id=0, has_side_effects=True, vmem_limit_bytes=48 * 1024 * 1024),
    )(v, mhi, mlo, geo, mw, snap, elem_map, eigvecs, sel)
    return out[:per_sec, : modes // nblk]


def solution(mesh):
    placed = (
        P(None, None, ("sec", "blk"), None),
        P(None, ("sec", "blk"), None),
        P(("sec", "blk"), None),
        P(None, None, ("sec", "blk"), None),
        P("blk", None),
        P(),
        P(("sec", "blk")),
    )
    return jax.shard_map(
        shards, mesh=mesh, in_specs=placed, out_specs=P("sec", "blk"), check_vma=False
    )
```

```python
import functools
import math

import jax
import jax.numpy as jnp
import numpy as np
from jax import lax
from jax.experimental import pallas as pl
from jax.experimental.pallas import tpu as pltpu
from jax.sharding import PartitionSpec as P

GLL_NODES = np.array(
    [
        -1.0,
        -0.8717401485096066,
        -0.5917001814331423,
        -0.2092992179024789,
        0.2092992179024789,
        0.5917001814331423,
        0.8717401485096066,
        1.0,
    ]
)
GLL_WEIGHTS = np.array(
    [
        1.0 / 28.0,
        0.2107042271435061,
        0.3411226924835044,
        0.4124587946587038,
        0.4124587946587038,
        0.3411226924835044,
        0.2107042271435061,
        1.0 / 28.0,
    ]
)


def legendre_seven(nodes):
    before = nodes * 0.0 + 1.0
    current = nodes * 1.0
    for order in range(1, 7):
        following = ((2.0 * order + 1.0) * nodes * current - order * before) / (order + 1.0)
        before = current
        current = following
    return current


def derivative_matrix():
    degree = 7
    values = legendre_seven(GLL_NODES)
    result = np.zeros((8, 8))
    for row_idx in range(8):
        for col_idx in range(8):
            if row_idx != col_idx:
                result[row_idx, col_idx] = values[row_idx] / (
                    values[col_idx] * (GLL_NODES[row_idx] - GLL_NODES[col_idx])
                )
    result[0, 0] = -degree * (degree + 1) / 4.0
    result[7, 7] = degree * (degree + 1) / 4.0
    return result.astype(np.float32)


def point_weights():
    cube = GLL_WEIGHTS[:, None, None] * GLL_WEIGHTS[None, :, None] * GLL_WEIGHTS[None, None, :]
    return cube.reshape(512).astype(np.float32)


MESH_IDS = pl.DeviceIdType.MESH
F32 = jnp.float32
BF16 = jnp.bfloat16


def kron_matrices():
    dt = derivative_matrix().astype(np.float64).T
    eye8 = np.eye(8)
    along_r = np.kron(dt, np.eye(64))
    along_s = np.kron(eye8, np.kron(dt, eye8))
    along_t = np.kron(np.eye(64), dt)
    full = np.concatenate([along_r, along_s, along_t], axis=1).astype(np.float32)
    upper = jnp.asarray(full).astype(BF16)
    lower = (jnp.asarray(full) - upper.astype(F32)).astype(BF16)
    return upper, lower


def split_dot(a, b):
    a_hi = a.astype(BF16)
    a_lo = (a - a_hi.astype(F32)).astype(BF16)
    b_hi = b.astype(BF16)
    b_lo = (b - b_hi.astype(F32)).astype(BF16)
    out = jnp.dot(a_hi, b_hi, preferred_element_type=F32)
    out = out + jnp.dot(a_hi, b_lo, preferred_element_type=F32)
    return out + jnp.dot(a_lo, b_hi, preferred_element_type=F32)


def exact_select(a, onehot):
    hi = a.astype(BF16)
    rest = a - hi.astype(F32)
    mid = rest.astype(BF16)
    lo = (rest - mid.astype(F32)).astype(BF16)
    out = jnp.dot(hi, onehot, preferred_element_type=F32)
    out = out + jnp.dot(mid, onehot, preferred_element_type=F32)
    return out + jnp.dot(lo, onehot, preferred_element_type=F32)


def comm_kernel(nsec, nblk, factor, v_ref, mhi_ref, mlo_ref, geo_ref, mass_ref, w_ref, snap_ref,
                em_ref, e_ref, mo_ref, out_ref,
                cin, r1, eg, s2, r2, s3, r3, deriv, ss1, rs1, sse, rse, ss2, rs2, ss3, rs3):
    s = lax.axis_index("sec")
    b = lax.axis_index("blk")

    barrier = pltpu.get_barrier_semaphore()

    def greet_sec(d, c):
        peer = lax.rem(s + d, nsec)
        pl.semaphore_signal(barrier, 1, device_id=(peer, b), device_id_type=MESH_IDS)
        return c

    def greet_blk(d, c):
        peer = lax.rem(b + d, nblk)
        pl.semaphore_signal(barrier, 1, device_id=(s, peer), device_id_type=MESH_IDS)
        return c

    lax.fori_loop(1, nsec, greet_sec, 0)
    lax.fori_loop(1, nblk, greet_blk, 0)

    rows_v, pts = v_ref.shape
    comps = 3
    elems = mass_ref.shape[0]
    fields = rows_v // (comps * elems)
    v = v_ref[...]
    deriv[...] = (jnp.dot(v, mhi_ref[...], preferred_element_type=F32)
                  + jnp.dot(v, mlo_ref[...], preferred_element_type=F32))

    def along(a, c, e):
        row = (c * elems + e) * fields
        return deriv[row:row + fields, a * pts:(a + 1) * pts]

    weighted = []
    for e in range(elems):
        def geo(k):
            return geo_ref[k, e:e + 1, :]

        def gradient(c, coord):
            return (geo(coord) * along(0, c, e) + geo(3 + coord) * along(1, c, e)
                    + geo(6 + coord) * along(2, c, e))

        scale = mass_ref[e:e + 1, :] * w_ref[...]
        vort = [gradient(2, 1) - gradient(1, 2), gradient(0, 2) - gradient(2, 0),
                gradient(1, 0) - gradient(0, 1)]
        weighted.append([(scale * x).astype(BF16) for x in vort])

    local = jnp.zeros((fields, snap_ref.shape[1]), F32)
    for c in range(comps):
        for j in range(elems):
            stored = jnp.zeros_like(weighted[0][c])
            for e in range(elems):
                stored = jnp.where(em_ref[e] == j, weighted[e][c], stored)
            local = local + lax.dot_general(
                stored, snap_ref[c * elems + j], (((1,), (1,)), ((), ())),
                preferred_element_type=F32)

    per_sec = fields // nsec
    lanes = 128
    chunks = local.shape[1] // lanes
    for j in range(nsec):
        for qq in range(chunks):
            cin[j, qq * per_sec:(qq + 1) * per_sec, :] = local[
                j * per_sec:(j + 1) * per_sec, qq * lanes:(qq + 1) * lanes]

    pl.semaphore_wait(barrier, (nsec - 1) + (nblk - 1))

    zc = 4
    y = b // (2 * zc)
    z_hi = lax.rem(b // 2, zc)
    core = lax.rem(b, 2)
    g = y * 2 + core
    ng = nblk // zc

    def g_device(gp):
        return (gp // 2) * (2 * zc) + z_hi * 2 + lax.rem(gp, 2)

    def z_device(zp):
        return y * (2 * zc) + zp * 2 + core

    def sec_copy(j, dst):
        return pltpu.make_async_remote_copy(
            cin.at[j], r1.at[dst], ss1.at[j], rs1.at[dst],
            device_id=(j, b), device_id_type=MESH_IDS)

    def e_copy(zp, slot):
        return pltpu.make_async_remote_copy(
            e_ref, eg.at[slot], sse.at[zp], rse.at[slot],
            device_id=(s, z_device(zp)), device_id_type=MESH_IDS)

    def g_copy(gp, slot):
        return pltpu.make_async_remote_copy(
            s2.at[gp], r2.at[slot], ss2.at[gp], rs2.at[slot],
            device_id=(s, g_device(gp)), device_id_type=MESH_IDS)

    def blk_copy(j, slot):
        return pltpu.make_async_remote_copy(
            s3.at[j], r3.at[slot], ss3.at[j], rs3.at[slot],
            device_id=(s, j), device_id_type=MESH_IDS)

    def over(n, me, fn):
        def body(d, c):
            fn(lax.rem(me + d, n))
            return c
        lax.fori_loop(1, n, body, 0)

    def reduce(n, me, wait, recv, acc):
        def body(d, a):
            j = lax.rem(me + d, n)
            wait(j)
            return a + recv[j]
        return lax.fori_loop(1, n, body, acc)

    over(zc, z_hi, lambda zp: e_copy(zp, z_hi).start())
    over(nsec, s, lambda j: sec_copy(j, s).start())
    cb = reduce(nsec, s, lambda j: sec_copy(j, j).wait_recv(), r1, cin[s])

    modes = e_ref.shape[1]
    width = 128
    per_sec = s2.shape[1]
    m_total = (cb.shape[0] // per_sec) * width
    rows = m_total // nblk
    lane_group = lax.broadcasted_iota(jnp.int32, (per_sec, width), 1) // rows
    for gp in range(ng):
        packed = jnp.zeros((per_sec, width), F32)
        for zp in range(zc):
            block = (gp // 2) * (2 * zc) + zp * 2 + gp % 2
            qq = (block * rows) // width
            window = cb[qq * per_sec:(qq + 1) * per_sec, :]
            shift = (rows * zp - (block * rows - qq * width)) % width
            moved = pltpu.roll(window, shift, 1) if shift else window
            packed = jnp.where(lane_group == zp, moved, packed)
        s2[gp] = packed
    over(ng, g, lambda gp: g_copy(gp, g).start())

    eg[z_hi] = e_ref[...]
    over(zc, z_hi, lambda zp: e_copy(zp, zp).wait_recv())
    cp = reduce(ng, g, lambda gp: g_copy(gp, gp).wait_recv(), r2, s2[g])
    sel = (lax.broadcasted_iota(jnp.int32, (modes, modes), 0) == mo_ref[...]).astype(BF16)
    e_part = exact_select(eg[...].reshape(zc * e_ref.shape[0], modes), sel)
    q = split_dot(cp[:, 0:zc * rows], e_part)

    step = modes // nblk
    per_window = width // step
    for j in range(nblk):
        window = q[:, (j // per_window) * width:(j // per_window + 1) * width]
        shift = (width - step * (j % per_window)) % width
        s3[j] = pltpu.roll(window, shift, 1) if shift else window
    over(nblk, b, lambda j: blk_copy(j, b).start())
    over(nsec, s, lambda j: sec_copy(j, s).wait_send())
    over(zc, z_hi, lambda zp: e_copy(zp, z_hi).wait_send())
    over(ng, g, lambda gp: g_copy(gp, g).wait_send())
    total = reduce(nblk, b, lambda j: blk_copy(j, j).wait_recv(), r3, s3[b])
    out_ref[...] = total[0:out_ref.shape[0], 0:out_ref.shape[1]] * factor
    over(nblk, b, lambda j: blk_copy(j, b).wait_send())


def shards(velocity, geometry, mass, snapshots, eigvecs, mode_order, elem_map):
    nsec = lax.axis_size("sec")
    nblk = lax.axis_size("blk")
    fields, comps, elems, pts = velocity.shape
    m_count = snapshots.shape[0]
    v = jnp.transpose(velocity, (1, 2, 0, 3)).reshape(comps * elems * fields, pts)
    snap = jnp.transpose(snapshots, (1, 2, 0, 3)).reshape(comps * elems, m_count, pts)
    weights = jnp.asarray(point_weights()).reshape(1, pts)
    modes = eigvecs.shape[1]
    mhi, mlo = kron_matrices()
    per_sec = fields // nsec
    chunks = m_count // 128
    factor = 0.25 / math.sqrt(elems * nsec * nblk)
    kernel = functools.partial(comm_kernel, nsec, nblk, factor)
    tile = (nblk, per_sec, 128)
    vmem = pl.BlockSpec(memory_space=pltpu.VMEM)
    out = pl.pallas_call(
        kernel,
        out_shape=jax.ShapeDtypeStruct((per_sec, modes // nblk), F32),
        in_specs=[vmem] * 7 + [pl.BlockSpec(memory_space=pltpu.SMEM)] + [vmem] * 2,
        out_specs=vmem,
        scratch_shapes=[
            pltpu.VMEM((nsec, chunks * per_sec, 128), F32),
            pltpu.VMEM((nsec, chunks * per_sec, 128), F32),
            pltpu.VMEM((4,) + eigvecs.shape, F32),
            pltpu.VMEM((nblk // 4, per_sec, 128), F32),
            pltpu.VMEM((nblk // 4, per_sec, 128), F32),
            pltpu.VMEM(tile, F32),
            pltpu.VMEM(tile, F32),
            pltpu.VMEM((comps * elems * fields, 3 * pts), F32),
            pltpu.SemaphoreType.DMA((nsec,)),
            pltpu.SemaphoreType.DMA((nsec,)),
            pltpu.SemaphoreType.DMA((4,)),
            pltpu.SemaphoreType.DMA((4,)),
            pltpu.SemaphoreType.DMA((nblk // 4,)),
            pltpu.SemaphoreType.DMA((nblk // 4,)),
            pltpu.SemaphoreType.DMA((nblk,)),
            pltpu.SemaphoreType.DMA((nblk,)),
        ],
        compiler_params=pltpu.CompilerParams(
            collective_id=0, has_side_effects=True, vmem_limit_bytes=48 * 1024 * 1024),
    )(v, mhi, mlo, geometry, mass, weights, snap, elem_map, eigvecs, mode_order.reshape(1, modes))
    return out


def solution(mesh):
    placed = (
        P(None, None, ("sec", "blk"), None),
        P(None, ("sec", "blk"), None),
        P(("sec", "blk"), None),
        P(None, None, ("sec", "blk"), None),
        P("blk", None),
        P(),
        P(("sec", "blk")),
    )
    return jax.shard_map(
        shards, mesh=mesh, in_specs=placed, out_specs=P("sec", "blk"), check_vma=False
    )
```

```python
import functools
import math

import jax
import jax.numpy as jnp
import numpy as np
from jax import lax
from jax.experimental import pallas as pl
from jax.experimental.pallas import tpu as pltpu
from jax.sharding import PartitionSpec as P

GLL_NODES = np.array(
    [
        -1.0,
        -0.8717401485096066,
        -0.5917001814331423,
        -0.2092992179024789,
        0.2092992179024789,
        0.5917001814331423,
        0.8717401485096066,
        1.0,
    ]
)
GLL_WEIGHTS = np.array(
    [
        1.0 / 28.0,
        0.2107042271435061,
        0.3411226924835044,
        0.4124587946587038,
        0.4124587946587038,
        0.3411226924835044,
        0.2107042271435061,
        1.0 / 28.0,
    ]
)


def legendre_seven(nodes):
    before = nodes * 0.0 + 1.0
    current = nodes * 1.0
    for order in range(1, 7):
        following = ((2.0 * order + 1.0) * nodes * current - order * before) / (order + 1.0)
        before = current
        current = following
    return current


def derivative_matrix():
    degree = 7
    values = legendre_seven(GLL_NODES)
    result = np.zeros((8, 8))
    for row_idx in range(8):
        for col_idx in range(8):
            if row_idx != col_idx:
                result[row_idx, col_idx] = values[row_idx] / (
                    values[col_idx] * (GLL_NODES[row_idx] - GLL_NODES[col_idx])
                )
    result[0, 0] = -degree * (degree + 1) / 4.0
    result[7, 7] = degree * (degree + 1) / 4.0
    return result.astype(np.float32)


def point_weights():
    cube = GLL_WEIGHTS[:, None, None] * GLL_WEIGHTS[None, :, None] * GLL_WEIGHTS[None, None, :]
    return cube.reshape(512).astype(np.float32)


MESH_IDS = pl.DeviceIdType.MESH
F32 = jnp.float32
BF16 = jnp.bfloat16


def kron_matrices():
    dt = lax.optimization_barrier(jnp.asarray(derivative_matrix().T))
    eye8 = jnp.eye(8, dtype=F32)
    along = [
        jnp.kron(dt, jnp.eye(64, dtype=F32)),
        jnp.kron(eye8, jnp.kron(dt, eye8)),
        jnp.kron(jnp.eye(64, dtype=F32), dt),
    ]
    parts = []
    for full in along:
        upper = full.astype(BF16)
        parts += [upper, (full - upper.astype(F32)).astype(BF16)]
    return parts


def split_dot(a, b):
    a_hi = a.astype(BF16)
    a_lo = (a - a_hi.astype(F32)).astype(BF16)
    b_hi = b.astype(BF16)
    b_lo = (b - b_hi.astype(F32)).astype(BF16)
    out = jnp.dot(a_hi, b_hi, preferred_element_type=F32)
    out = out + jnp.dot(a_hi, b_lo, preferred_element_type=F32)
    return out + jnp.dot(a_lo, b_hi, preferred_element_type=F32)


def exact_select(a, onehot):
    hi = a.astype(BF16)
    rest = a - hi.astype(F32)
    mid = rest.astype(BF16)
    lo = (rest - mid.astype(F32)).astype(BF16)
    out = jnp.dot(hi, onehot, preferred_element_type=F32)
    out = out + jnp.dot(mid, onehot, preferred_element_type=F32)
    return out + jnp.dot(lo, onehot, preferred_element_type=F32)


def comm_kernel(nsec, nblk, factor, v_ref, mr_hi, mr_lo, ms_hi, ms_lo, mt_hi, mt_lo, geo_ref, mass_ref, w_ref, snap_ref,
                em_ref, e_ref, mo_ref, out_ref,
                cin, r1, eg, s2, r2, s3, r3, deriv, ss1, rs1, sse, rse, ss2, rs2, ss3, rs3):
    s = lax.axis_index("sec")
    b = lax.axis_index("blk")

    barrier = pltpu.get_barrier_semaphore()

    def greet_sec(d, c):
        peer = lax.rem(s + d, nsec)
        pl.semaphore_signal(barrier, 1, device_id=(peer, b), device_id_type=MESH_IDS)
        return c

    def greet_blk(d, c):
        peer = lax.rem(b + d, nblk)
        pl.semaphore_signal(barrier, 1, device_id=(s, peer), device_id_type=MESH_IDS)
        return c

    lax.fori_loop(1, nsec, greet_sec, 0)
    lax.fori_loop(1, nblk, greet_blk, 0)

    fields, comps, elems, pts = v_ref.shape
    v = jnp.concatenate([v_ref[:, c, e, :] for c in range(3) for e in range(mass_ref.shape[0])], axis=0)
    for a, (m_hi, m_lo) in enumerate(((mr_hi, mr_lo), (ms_hi, ms_lo), (mt_hi, mt_lo))):
        deriv[:, a * pts:(a + 1) * pts] = (
            jnp.dot(v, m_hi[...], preferred_element_type=F32)
            + jnp.dot(v, m_lo[...], preferred_element_type=F32))

    def along(a, c, e):
        row = (c * elems + e) * fields
        return deriv[row:row + fields, a * pts:(a + 1) * pts]

    weighted = []
    for e in range(elems):
        def geo(k):
            return geo_ref[k, e:e + 1, :]

        def gradient(c, coord):
            return (geo(coord) * along(0, c, e) + geo(3 + coord) * along(1, c, e)
                    + geo(6 + coord) * along(2, c, e))

        scale = mass_ref[e:e + 1, :] * w_ref[...]
        vort = [gradient(2, 1) - gradient(1, 2), gradient(0, 2) - gradient(2, 0),
                gradient(1, 0) - gradient(0, 1)]
        weighted.append([(scale * x).astype(BF16) for x in vort])

    local = jnp.zeros((fields, snap_ref.shape[0]), F32)
    for c in range(comps):
        for j in range(elems):
            stored = jnp.zeros_like(weighted[0][c])
            for e in range(elems):
                stored = jnp.where(em_ref[e] == j, weighted[e][c], stored)
            local = local + lax.dot_general(
                stored, snap_ref[:, c, j, :], (((1,), (1,)), ((), ())),
                preferred_element_type=F32)

    per_sec = fields // nsec
    lanes = 128
    chunks = local.shape[1] // lanes
    for j in range(nsec):
        for qq in range(chunks):
            cin[j, qq * per_sec:(qq + 1) * per_sec, :] = local[
                j * per_sec:(j + 1) * per_sec, qq * lanes:(qq + 1) * lanes]

    pl.semaphore_wait(barrier, (nsec - 1) + (nblk - 1))

    zc = 4
    y = b // (2 * zc)
    z_hi = lax.rem(b // 2, zc)
    core = lax.rem(b, 2)
    g = y * 2 + core
    ng = nblk // zc

    def g_device(gp):
        return (gp // 2) * (2 * zc) + z_hi * 2 + lax.rem(gp, 2)

    def z_device(zp):
        return y * (2 * zc) + zp * 2 + core

    def sec_copy(j, dst):
        return pltpu.make_async_remote_copy(
            cin.at[j], r1.at[dst], ss1.at[j], rs1.at[dst],
            device_id=(j, b), device_id_type=MESH_IDS)

    def e_copy(zp, slot):
        return pltpu.make_async_remote_copy(
            e_ref, eg.at[slot], sse.at[zp], rse.at[slot],
            device_id=(s, z_device(zp)), device_id_type=MESH_IDS)

    def g_copy(gp, slot):
        return pltpu.make_async_remote_copy(
            s2.at[gp], r2.at[slot], ss2.at[gp], rs2.at[slot],
            device_id=(s, g_device(gp)), device_id_type=MESH_IDS)

    def blk_copy(j, slot):
        return pltpu.make_async_remote_copy(
            s3.at[j], r3.at[slot], ss3.at[j], rs3.at[slot],
            device_id=(s, j), device_id_type=MESH_IDS)

    def over(n, me, fn):
        def body(d, c):
            fn(lax.rem(me + d, n))
            return c
        lax.fori_loop(1, n, body, 0)

    def reduce(n, me, wait, recv, acc):
        def body(d, a):
            j = lax.rem(me + d, n)
            wait(j)
            return a + recv[j]
        return lax.fori_loop(1, n, body, acc)

    over(zc, z_hi, lambda zp: e_copy(zp, z_hi).start())
    over(nsec, s, lambda j: sec_copy(j, s).start())
    cb = reduce(nsec, s, lambda j: sec_copy(j, j).wait_recv(), r1, cin[s])

    modes = e_ref.shape[1]
    width = 128
    per_sec = s2.shape[1]
    m_total = (cb.shape[0] // per_sec) * width
    rows = m_total // nblk
    lane_group = lax.broadcasted_iota(jnp.int32, (per_sec, width), 1) // rows
    for gp in range(ng):
        packed = jnp.zeros((per_sec, width), F32)
        for zp in range(zc):
            block = (gp // 2) * (2 * zc) + zp * 2 + gp % 2
            qq = (block * rows) // width
            window = cb[qq * per_sec:(qq + 1) * per_sec, :]
            shift = (rows * zp - (block * rows - qq * width)) % width
            moved = pltpu.roll(window, shift, 1) if shift else window
            packed = jnp.where(lane_group == zp, moved, packed)
        s2[gp] = packed
    over(ng, g, lambda gp: g_copy(gp, g).start())

    eg[z_hi] = e_ref[...]
    over(zc, z_hi, lambda zp: e_copy(zp, zp).wait_recv())
    cp = reduce(ng, g, lambda gp: g_copy(gp, gp).wait_recv(), r2, s2[g])
    sel = (lax.broadcasted_iota(jnp.int32, (modes, modes), 0) == mo_ref[...]).astype(BF16)
    e_part = exact_select(eg[...].reshape(zc * e_ref.shape[0], modes), sel)
    q = split_dot(cp[:, 0:zc * rows], e_part)

    step = modes // nblk
    per_window = width // step
    for j in range(nblk):
        window = q[:, (j // per_window) * width:(j // per_window + 1) * width]
        shift = (width - step * (j % per_window)) % width
        s3[j] = pltpu.roll(window, shift, 1) if shift else window
    over(nblk, b, lambda j: blk_copy(j, b).start())
    over(nsec, s, lambda j: sec_copy(j, s).wait_send())
    over(zc, z_hi, lambda zp: e_copy(zp, z_hi).wait_send())
    over(ng, g, lambda gp: g_copy(gp, g).wait_send())
    total = reduce(nblk, b, lambda j: blk_copy(j, j).wait_recv(), r3, s3[b])
    out_ref[...] = total[0:out_ref.shape[0], 0:out_ref.shape[1]] * factor
    over(nblk, b, lambda j: blk_copy(j, b).wait_send())


def shards(velocity, geometry, mass, snapshots, eigvecs, mode_order, elem_map):
    nsec = lax.axis_size("sec")
    nblk = lax.axis_size("blk")
    fields, comps, elems, pts = velocity.shape
    m_count = snapshots.shape[0]
    weights = jnp.asarray(point_weights()).reshape(1, pts)
    modes = eigvecs.shape[1]
    mats = kron_matrices()
    per_sec = fields // nsec
    chunks = m_count // 128
    factor = 0.25 / math.sqrt(elems * nsec * nblk)
    kernel = functools.partial(comm_kernel, nsec, nblk, factor)
    tile = (nblk, per_sec, 128)
    vmem = pl.BlockSpec(memory_space=pltpu.VMEM)
    out = pl.pallas_call(
        kernel,
        out_shape=jax.ShapeDtypeStruct((per_sec, modes // nblk), F32),
        in_specs=[vmem] * 11 + [pl.BlockSpec(memory_space=pltpu.SMEM)] + [vmem] * 2,
        out_specs=vmem,
        scratch_shapes=[
            pltpu.VMEM((nsec, chunks * per_sec, 128), F32),
            pltpu.VMEM((nsec, chunks * per_sec, 128), F32),
            pltpu.VMEM((4,) + eigvecs.shape, F32),
            pltpu.VMEM((nblk // 4, per_sec, 128), F32),
            pltpu.VMEM((nblk // 4, per_sec, 128), F32),
            pltpu.VMEM(tile, F32),
            pltpu.VMEM(tile, F32),
            pltpu.VMEM((comps * elems * fields, 3 * pts), F32),
            pltpu.SemaphoreType.DMA((nsec,)),
            pltpu.SemaphoreType.DMA((nsec,)),
            pltpu.SemaphoreType.DMA((4,)),
            pltpu.SemaphoreType.DMA((4,)),
            pltpu.SemaphoreType.DMA((nblk // 4,)),
            pltpu.SemaphoreType.DMA((nblk // 4,)),
            pltpu.SemaphoreType.DMA((nblk,)),
            pltpu.SemaphoreType.DMA((nblk,)),
        ],
        compiler_params=pltpu.CompilerParams(
            collective_id=0, has_side_effects=True, vmem_limit_bytes=48 * 1024 * 1024),
    )(velocity, *mats, geometry, mass, weights, snapshots, elem_map, eigvecs, mode_order.reshape(1, modes))
    return out


def solution(mesh):
    placed = (
        P(None, None, ("sec", "blk"), None),
        P(None, ("sec", "blk"), None),
        P(("sec", "blk"), None),
        P(None, None, ("sec", "blk"), None),
        P("blk", None),
        P(),
        P(("sec", "blk")),
    )
    return jax.shard_map(
        shards, mesh=mesh, in_specs=placed, out_specs=P("sec", "blk"), check_vma=False
    )
```

```python
import functools
import math

import ml_dtypes

import jax
import jax.numpy as jnp
import numpy as np
from jax import lax
from jax.experimental import pallas as pl
from jax.experimental.pallas import tpu as pltpu
from jax.sharding import PartitionSpec as P

GLL_NODES = np.array(
    [
        -1.0,
        -0.8717401485096066,
        -0.5917001814331423,
        -0.2092992179024789,
        0.2092992179024789,
        0.5917001814331423,
        0.8717401485096066,
        1.0,
    ]
)
GLL_WEIGHTS = np.array(
    [
        1.0 / 28.0,
        0.2107042271435061,
        0.3411226924835044,
        0.4124587946587038,
        0.4124587946587038,
        0.3411226924835044,
        0.2107042271435061,
        1.0 / 28.0,
    ]
)


def legendre_seven(nodes):
    before = nodes * 0.0 + 1.0
    current = nodes * 1.0
    for order in range(1, 7):
        following = ((2.0 * order + 1.0) * nodes * current - order * before) / (order + 1.0)
        before = current
        current = following
    return current


def derivative_matrix():
    degree = 7
    values = legendre_seven(GLL_NODES)
    result = np.zeros((8, 8))
    for row_idx in range(8):
        for col_idx in range(8):
            if row_idx != col_idx:
                result[row_idx, col_idx] = values[row_idx] / (
                    values[col_idx] * (GLL_NODES[row_idx] - GLL_NODES[col_idx])
                )
    result[0, 0] = -degree * (degree + 1) / 4.0
    result[7, 7] = degree * (degree + 1) / 4.0
    return result.astype(np.float32)


def point_weights():
    cube = GLL_WEIGHTS[:, None, None] * GLL_WEIGHTS[None, :, None] * GLL_WEIGHTS[None, None, :]
    return cube.reshape(512).astype(np.float32)


MESH_IDS = pl.DeviceIdType.MESH
F32 = jnp.float32
BF16 = jnp.bfloat16


def host_split(full):
    upper = full.astype(ml_dtypes.bfloat16)
    lower = (full - upper.astype(np.float32)).astype(ml_dtypes.bfloat16)
    return jnp.asarray(upper), jnp.asarray(lower)


def kron_matrices():
    dt = derivative_matrix().astype(np.float64).T
    eye8 = np.eye(8)
    along_r = np.kron(dt, np.eye(64)).astype(np.float32)
    pair = np.eye(2)
    along_st = np.concatenate(
        [np.kron(pair, np.kron(dt, eye8)), np.kron(pair, np.kron(eye8, dt))], axis=1
    ).astype(np.float32)
    return host_split(along_r) + host_split(along_st)


def split_dot(a, b):
    a_hi = a.astype(BF16)
    a_lo = (a - a_hi.astype(F32)).astype(BF16)
    b_hi = b.astype(BF16)
    b_lo = (b - b_hi.astype(F32)).astype(BF16)
    out = jnp.dot(a_hi, b_hi, preferred_element_type=F32)
    out = out + jnp.dot(a_hi, b_lo, preferred_element_type=F32)
    return out + jnp.dot(a_lo, b_hi, preferred_element_type=F32)


def exact_select(a, onehot):
    hi = a.astype(BF16)
    rest = a - hi.astype(F32)
    mid = rest.astype(BF16)
    lo = (rest - mid.astype(F32)).astype(BF16)
    out = jnp.dot(hi, onehot, preferred_element_type=F32)
    out = out + jnp.dot(mid, onehot, preferred_element_type=F32)
    return out + jnp.dot(lo, onehot, preferred_element_type=F32)


def comm_kernel(nsec, nblk, factor, v_ref, mr_hi, mr_lo, st_hi, st_lo, geo_ref, mass_ref, w_ref, snap_ref,
                em_ref, e_ref, mo_ref, out_ref,
                cin, r1, eg, s2, r2, s3, r3, deriv, ss1, rs1, sse, rse, ss2, rs2, ss3, rs3):
    s = lax.axis_index("sec")
    b = lax.axis_index("blk")

    barrier = pltpu.get_barrier_semaphore()

    def greet_sec(d, c):
        peer = lax.rem(s + d, nsec)
        pl.semaphore_signal(barrier, 1, device_id=(peer, b), device_id_type=MESH_IDS)
        return c

    def greet_blk(d, c):
        peer = lax.rem(b + d, nblk)
        pl.semaphore_signal(barrier, 1, device_id=(s, peer), device_id_type=MESH_IDS)
        return c

    lax.fori_loop(1, nsec, greet_sec, 0)
    lax.fori_loop(1, nblk, greet_blk, 0)

    fields, comps, elems, pts = v_ref.shape
    v = jnp.concatenate([v_ref[:, c, e, :] for c in range(3) for e in range(mass_ref.shape[0])], axis=0)
    deriv[:, 0:pts] = (jnp.dot(v, mr_hi[...], preferred_element_type=F32)
                       + jnp.dot(v, mr_lo[...], preferred_element_type=F32))
    chunk = st_hi.shape[0]
    for c in range(pts // chunk):
        part = v[:, c * chunk:(c + 1) * chunk]
        both = (jnp.dot(part, st_hi[...], preferred_element_type=F32)
                + jnp.dot(part, st_lo[...], preferred_element_type=F32))
        deriv[:, pts + c * chunk:pts + (c + 1) * chunk] = both[:, 0:chunk]
        deriv[:, 2 * pts + c * chunk:2 * pts + (c + 1) * chunk] = both[:, chunk:2 * chunk]

    def along(a, c, e):
        row = (c * elems + e) * fields
        return deriv[row:row + fields, a * pts:(a + 1) * pts]

    weighted = []
    for e in range(elems):
        def geo(k):
            return geo_ref[k, e:e + 1, :]

        def gradient(c, coord):
            return (geo(coord) * along(0, c, e) + geo(3 + coord) * along(1, c, e)
                    + geo(6 + coord) * along(2, c, e))

        scale = mass_ref[e:e + 1, :] * w_ref[...]
        vort = [gradient(2, 1) - gradient(1, 2), gradient(0, 2) - gradient(2, 0),
                gradient(1, 0) - gradient(0, 1)]
        weighted.append([(scale * x).astype(BF16) for x in vort])

    local = jnp.zeros((fields, snap_ref.shape[0]), F32)
    for c in range(comps):
        for j in range(elems):
            stored = jnp.zeros_like(weighted[0][c])
            for e in range(elems):
                stored = jnp.where(em_ref[e] == j, weighted[e][c], stored)
            local = local + lax.dot_general(
                stored, snap_ref[:, c, j, :], (((1,), (1,)), ((), ())),
                preferred_element_type=F32)

    per_sec = fields // nsec
    lanes = 128
    chunks = local.shape[1] // lanes
    for j in range(nsec):
        for qq in range(chunks):
            cin[j, qq * per_sec:(qq + 1) * per_sec, :] = local[
                j * per_sec:(j + 1) * per_sec, qq * lanes:(qq + 1) * lanes]

    pl.semaphore_wait(barrier, (nsec - 1) + (nblk - 1))

    zc = 4
    y = b // (2 * zc)
    z_hi = lax.rem(b // 2, zc)
    core = lax.rem(b, 2)
    g = y * 2 + core
    ng = nblk // zc

    def g_device(gp):
        return (gp // 2) * (2 * zc) + z_hi * 2 + lax.rem(gp, 2)

    def z_device(zp):
        return y * (2 * zc) + zp * 2 + core

    def sec_copy(j, dst):
        return pltpu.make_async_remote_copy(
            cin.at[j], r1.at[dst], ss1.at[j], rs1.at[dst],
            device_id=(j, b), device_id_type=MESH_IDS)

    def e_copy(zp, slot):
        return pltpu.make_async_remote_copy(
            e_ref, eg.at[slot], sse.at[zp], rse.at[slot],
            device_id=(s, z_device(zp)), device_id_type=MESH_IDS)

    def g_copy(gp, slot):
        return pltpu.make_async_remote_copy(
            s2.at[gp], r2.at[slot], ss2.at[gp], rs2.at[slot],
            device_id=(s, g_device(gp)), device_id_type=MESH_IDS)

    def blk_copy(j, slot):
        return pltpu.make_async_remote_copy(
            s3.at[j], r3.at[slot], ss3.at[j], rs3.at[slot],
            device_id=(s, j), device_id_type=MESH_IDS)

    def over(n, me, fn):
        def body(d, c):
            fn(lax.rem(me + d, n))
            return c
        lax.fori_loop(1, n, body, 0)

    def reduce(n, me, wait, recv, acc):
        def body(d, a):
            j = lax.rem(me + d, n)
            wait(j)
            return a + recv[j]
        return lax.fori_loop(1, n, body, acc)

    over(zc, z_hi, lambda zp: e_copy(zp, z_hi).start())
    over(nsec, s, lambda j: sec_copy(j, s).start())
    cb = reduce(nsec, s, lambda j: sec_copy(j, j).wait_recv(), r1, cin[s])

    modes = e_ref.shape[1]
    width = 128
    per_sec = s2.shape[1]
    m_total = (cb.shape[0] // per_sec) * width
    rows = m_total // nblk
    lane_group = lax.broadcasted_iota(jnp.int32, (per_sec, width), 1) // rows
    for gp in range(ng):
        packed = jnp.zeros((per_sec, width), F32)
        for zp in range(zc):
            block = (gp // 2) * (2 * zc) + zp * 2 + gp % 2
            qq = (block * rows) // width
            window = cb[qq * per_sec:(qq + 1) * per_sec, :]
            shift = (rows * zp - (block * rows - qq * width)) % width
            moved = pltpu.roll(window, shift, 1) if shift else window
            packed = jnp.where(lane_group == zp, moved, packed)
        s2[gp] = packed
    over(ng, g, lambda gp: g_copy(gp, g).start())

    eg[z_hi] = e_ref[...]
    over(zc, z_hi, lambda zp: e_copy(zp, zp).wait_recv())
    cp = reduce(ng, g, lambda gp: g_copy(gp, gp).wait_recv(), r2, s2[g])
    sel = (lax.broadcasted_iota(jnp.int32, (modes, modes), 0) == mo_ref[...]).astype(BF16)
    e_part = exact_select(eg[...].reshape(zc * e_ref.shape[0], modes), sel)
    q = split_dot(cp[:, 0:zc * rows], e_part)

    step = modes // nblk
    per_window = width // step
    for j in range(nblk):
        window = q[:, (j // per_window) * width:(j // per_window + 1) * width]
        shift = (width - step * (j % per_window)) % width
        s3[j] = pltpu.roll(window, shift, 1) if shift else window
    over(nblk, b, lambda j: blk_copy(j, b).start())
    over(nsec, s, lambda j: sec_copy(j, s).wait_send())
    over(zc, z_hi, lambda zp: e_copy(zp, z_hi).wait_send())
    over(ng, g, lambda gp: g_copy(gp, g).wait_send())
    total = reduce(nblk, b, lambda j: blk_copy(j, j).wait_recv(), r3, s3[b])
    out_ref[...] = total[0:out_ref.shape[0], 0:out_ref.shape[1]] * factor
    over(nblk, b, lambda j: blk_copy(j, b).wait_send())


def shards(velocity, geometry, mass, snapshots, eigvecs, mode_order, elem_map):
    nsec = lax.axis_size("sec")
    nblk = lax.axis_size("blk")
    fields, comps, elems, pts = velocity.shape
    m_count = snapshots.shape[0]
    weights = jnp.asarray(point_weights()).reshape(1, pts)
    modes = eigvecs.shape[1]
    mats = kron_matrices()
    per_sec = fields // nsec
    chunks = m_count // 128
    factor = 0.25 / math.sqrt(elems * nsec * nblk)
    kernel = functools.partial(comm_kernel, nsec, nblk, factor)
    tile = (nblk, per_sec, 128)
    vmem = pl.BlockSpec(memory_space=pltpu.VMEM)
    out = pl.pallas_call(
        kernel,
        out_shape=jax.ShapeDtypeStruct((per_sec, modes // nblk), F32),
        in_specs=[vmem] * 9 + [pl.BlockSpec(memory_space=pltpu.SMEM)] + [vmem] * 2,
        out_specs=vmem,
        scratch_shapes=[
            pltpu.VMEM((nsec, chunks * per_sec, 128), F32),
            pltpu.VMEM((nsec, chunks * per_sec, 128), F32),
            pltpu.VMEM((4,) + eigvecs.shape, F32),
            pltpu.VMEM((nblk // 4, per_sec, 128), F32),
            pltpu.VMEM((nblk // 4, per_sec, 128), F32),
            pltpu.VMEM(tile, F32),
            pltpu.VMEM(tile, F32),
            pltpu.VMEM((comps * elems * fields, 3 * pts), F32),
            pltpu.SemaphoreType.DMA((nsec,)),
            pltpu.SemaphoreType.DMA((nsec,)),
            pltpu.SemaphoreType.DMA((4,)),
            pltpu.SemaphoreType.DMA((4,)),
            pltpu.SemaphoreType.DMA((nblk // 4,)),
            pltpu.SemaphoreType.DMA((nblk // 4,)),
            pltpu.SemaphoreType.DMA((nblk,)),
            pltpu.SemaphoreType.DMA((nblk,)),
        ],
        compiler_params=pltpu.CompilerParams(
            collective_id=0, has_side_effects=True, vmem_limit_bytes=48 * 1024 * 1024),
    )(velocity, *mats, geometry, mass, weights, snapshots, elem_map, eigvecs, mode_order.reshape(1, modes))
    return out


def solution(mesh):
    placed = (
        P(None, None, ("sec", "blk"), None),
        P(None, ("sec", "blk"), None),
        P(("sec", "blk"), None),
        P(None, None, ("sec", "blk"), None),
        P("blk", None),
        P(),
        P(("sec", "blk")),
    )
    return jax.shard_map(
        shards, mesh=mesh, in_specs=placed, out_specs=P("sec", "blk"), check_vma=False
    )
```

```python
import functools
import math

import ml_dtypes

import jax
import jax.numpy as jnp
import numpy as np
from jax import lax
from jax.experimental import pallas as pl
from jax.experimental.pallas import tpu as pltpu
from jax.sharding import PartitionSpec as P

GLL_NODES = np.array(
    [
        -1.0,
        -0.8717401485096066,
        -0.5917001814331423,
        -0.2092992179024789,
        0.2092992179024789,
        0.5917001814331423,
        0.8717401485096066,
        1.0,
    ]
)
GLL_WEIGHTS = np.array(
    [
        1.0 / 28.0,
        0.2107042271435061,
        0.3411226924835044,
        0.4124587946587038,
        0.4124587946587038,
        0.3411226924835044,
        0.2107042271435061,
        1.0 / 28.0,
    ]
)


def legendre_seven(nodes):
    before = nodes * 0.0 + 1.0
    current = nodes * 1.0
    for order in range(1, 7):
        following = ((2.0 * order + 1.0) * nodes * current - order * before) / (order + 1.0)
        before = current
        current = following
    return current


def derivative_matrix():
    degree = 7
    values = legendre_seven(GLL_NODES)
    result = np.zeros((8, 8))
    for row_idx in range(8):
        for col_idx in range(8):
            if row_idx != col_idx:
                result[row_idx, col_idx] = values[row_idx] / (
                    values[col_idx] * (GLL_NODES[row_idx] - GLL_NODES[col_idx])
                )
    result[0, 0] = -degree * (degree + 1) / 4.0
    result[7, 7] = degree * (degree + 1) / 4.0
    return result.astype(np.float32)


def point_weights():
    cube = GLL_WEIGHTS[:, None, None] * GLL_WEIGHTS[None, :, None] * GLL_WEIGHTS[None, None, :]
    return cube.reshape(512).astype(np.float32)


MESH_IDS = pl.DeviceIdType.MESH
F32 = jnp.float32
BF16 = jnp.bfloat16


def host_split(full):
    upper = full.astype(ml_dtypes.bfloat16)
    lower = (full - upper.astype(np.float32)).astype(ml_dtypes.bfloat16)
    return jnp.asarray(upper), jnp.asarray(lower)


def kron_matrices():
    dt = derivative_matrix().astype(np.float64).T
    eye8 = np.eye(8)
    along_r = np.kron(dt, np.eye(64)).astype(np.float32)
    pair = np.eye(2)
    along_st = np.concatenate(
        [np.kron(pair, np.kron(dt, eye8)), np.kron(pair, np.kron(eye8, dt))], axis=1
    ).astype(np.float32)
    return host_split(along_r) + host_split(along_st)


def split_dot(a, b):
    a_hi = a.astype(BF16)
    a_lo = (a - a_hi.astype(F32)).astype(BF16)
    b_hi = b.astype(BF16)
    b_lo = (b - b_hi.astype(F32)).astype(BF16)
    out = jnp.dot(a_hi, b_hi, preferred_element_type=F32)
    out = out + jnp.dot(a_hi, b_lo, preferred_element_type=F32)
    return out + jnp.dot(a_lo, b_hi, preferred_element_type=F32)


def exact_select(a, onehot):
    hi = a.astype(BF16)
    rest = a - hi.astype(F32)
    mid = rest.astype(BF16)
    lo = (rest - mid.astype(F32)).astype(BF16)
    out = jnp.dot(hi, onehot, preferred_element_type=F32)
    out = out + jnp.dot(mid, onehot, preferred_element_type=F32)
    return out + jnp.dot(lo, onehot, preferred_element_type=F32)


def comm_kernel(nsec, nblk, factor, v_hbm, mr_hi_hbm, mr_lo_hbm, st_hi_hbm, st_lo_hbm, geo_hbm,
                mass_hbm, w_hbm, snap_hbm, em_ref, e_hbm, mo_hbm, out_ref,
                mr_hi, mr_lo, st_hi, st_lo, geo_ref, mass_ref, w_ref, v_ref, snap_ref, e_ref, mo_ref, lsem,
                cin, r1, eg, s2, r2, s3, r3, deriv, ss1, rs1, sse, rse, ss2, rs2, ss3, rs3):
    s = lax.axis_index("sec")
    b = lax.axis_index("blk")

    loads = [
        pltpu.make_async_copy(src, dst, lsem.at[i])
        for i, (src, dst) in enumerate((
            (mr_hi_hbm, mr_hi), (mr_lo_hbm, mr_lo), (st_hi_hbm, st_hi), (st_lo_hbm, st_lo),
            (geo_hbm, geo_ref), (mass_hbm, mass_ref), (w_hbm, w_ref), (v_hbm, v_ref),
            (snap_hbm, snap_ref), (e_hbm, e_ref), (mo_hbm, mo_ref)))
    ]
    for load in loads:
        load.start()

    barrier = pltpu.get_barrier_semaphore()

    def greet_sec(d, c):
        peer = lax.rem(s + d, nsec)
        pl.semaphore_signal(barrier, 1, device_id=(peer, b), device_id_type=MESH_IDS)
        return c

    def greet_blk(d, c):
        peer = lax.rem(b + d, nblk)
        pl.semaphore_signal(barrier, 1, device_id=(s, peer), device_id_type=MESH_IDS)
        return c

    lax.fori_loop(1, nsec, greet_sec, 0)
    lax.fori_loop(1, nblk, greet_blk, 0)

    fields, comps, elems, pts = v_ref.shape
    for load in loads[:4] + loads[7:8]:
        load.wait()
    v = jnp.concatenate([v_ref[:, c, e, :] for c in range(3) for e in range(mass_ref.shape[0])], axis=0)
    deriv[:, 0:pts] = (jnp.dot(v, mr_hi[...], preferred_element_type=F32)
                       + jnp.dot(v, mr_lo[...], preferred_element_type=F32))
    chunk = st_hi.shape[0]
    for c in range(pts // chunk):
        part = v[:, c * chunk:(c + 1) * chunk]
        both = (jnp.dot(part, st_hi[...], preferred_element_type=F32)
                + jnp.dot(part, st_lo[...], preferred_element_type=F32))
        deriv[:, pts + c * chunk:pts + (c + 1) * chunk] = both[:, 0:chunk]
        deriv[:, 2 * pts + c * chunk:2 * pts + (c + 1) * chunk] = both[:, chunk:2 * chunk]

    def along(a, c, e):
        row = (c * elems + e) * fields
        return deriv[row:row + fields, a * pts:(a + 1) * pts]

    for load in loads[4:7]:
        load.wait()
    weighted = []
    for e in range(elems):
        def geo(k):
            return geo_ref[k, e:e + 1, :]

        def gradient(c, coord):
            return (geo(coord) * along(0, c, e) + geo(3 + coord) * along(1, c, e)
                    + geo(6 + coord) * along(2, c, e))

        scale = mass_ref[e:e + 1, :] * w_ref[...]
        vort = [gradient(2, 1) - gradient(1, 2), gradient(0, 2) - gradient(2, 0),
                gradient(1, 0) - gradient(0, 1)]
        weighted.append([(scale * x).astype(BF16) for x in vort])

    loads[8].wait()
    local = jnp.zeros((fields, snap_ref.shape[0]), F32)
    for c in range(comps):
        for j in range(elems):
            stored = jnp.zeros_like(weighted[0][c])
            for e in range(elems):
                stored = jnp.where(em_ref[e] == j, weighted[e][c], stored)
            local = local + lax.dot_general(
                stored, snap_ref[:, c, j, :], (((1,), (1,)), ((), ())),
                preferred_element_type=F32)

    per_sec = fields // nsec
    lanes = 128
    chunks = local.shape[1] // lanes
    for j in range(nsec):
        for qq in range(chunks):
            cin[j, qq * per_sec:(qq + 1) * per_sec, :] = local[
                j * per_sec:(j + 1) * per_sec, qq * lanes:(qq + 1) * lanes]

    for load in loads[9:]:
        load.wait()
    pl.semaphore_wait(barrier, (nsec - 1) + (nblk - 1))

    zc = 4
    y = b // (2 * zc)
    z_hi = lax.rem(b // 2, zc)
    core = lax.rem(b, 2)
    g = y * 2 + core
    ng = nblk // zc

    def g_device(gp):
        return (gp // 2) * (2 * zc) + z_hi * 2 + lax.rem(gp, 2)

    def z_device(zp):
        return y * (2 * zc) + zp * 2 + core

    def sec_copy(j, dst):
        return pltpu.make_async_remote_copy(
            cin.at[j], r1.at[dst], ss1.at[j], rs1.at[dst],
            device_id=(j, b), device_id_type=MESH_IDS)

    def e_copy(zp, slot):
        return pltpu.make_async_remote_copy(
            e_ref, eg.at[slot], sse.at[zp], rse.at[slot],
            device_id=(s, z_device(zp)), device_id_type=MESH_IDS)

    def g_copy(gp, slot):
        return pltpu.make_async_remote_copy(
            s2.at[gp], r2.at[slot], ss2.at[gp], rs2.at[slot],
            device_id=(s, g_device(gp)), device_id_type=MESH_IDS)

    def blk_copy(j, slot):
        return pltpu.make_async_remote_copy(
            s3.at[j], r3.at[slot], ss3.at[j], rs3.at[slot],
            device_id=(s, j), device_id_type=MESH_IDS)

    def over(n, me, fn):
        def body(d, c):
            fn(lax.rem(me + d, n))
            return c
        lax.fori_loop(1, n, body, 0)

    def reduce(n, me, wait, recv, acc):
        def body(d, a):
            j = lax.rem(me + d, n)
            wait(j)
            return a + recv[j]
        return lax.fori_loop(1, n, body, acc)

    over(zc, z_hi, lambda zp: e_copy(zp, z_hi).start())
    over(nsec, s, lambda j: sec_copy(j, s).start())
    cb = reduce(nsec, s, lambda j: sec_copy(j, j).wait_recv(), r1, cin[s])

    modes = e_ref.shape[1]
    width = 128
    per_sec = s2.shape[1]
    m_total = (cb.shape[0] // per_sec) * width
    rows = m_total // nblk
    lane_group = lax.broadcasted_iota(jnp.int32, (per_sec, width), 1) // rows
    for gp in range(ng):
        packed = jnp.zeros((per_sec, width), F32)
        for zp in range(zc):
            block = (gp // 2) * (2 * zc) + zp * 2 + gp % 2
            qq = (block * rows) // width
            window = cb[qq * per_sec:(qq + 1) * per_sec, :]
            shift = (rows * zp - (block * rows - qq * width)) % width
            moved = pltpu.roll(window, shift, 1) if shift else window
            packed = jnp.where(lane_group == zp, moved, packed)
        s2[gp] = packed
    over(ng, g, lambda gp: g_copy(gp, g).start())

    eg[z_hi] = e_ref[...]
    over(zc, z_hi, lambda zp: e_copy(zp, zp).wait_recv())
    cp = reduce(ng, g, lambda gp: g_copy(gp, gp).wait_recv(), r2, s2[g])
    sel = (lax.broadcasted_iota(jnp.int32, (modes, modes), 0) == mo_ref[...]).astype(BF16)
    e_part = exact_select(eg[...].reshape(zc * e_ref.shape[0], modes), sel)
    q = split_dot(cp[:, 0:zc * rows], e_part)

    step = modes // nblk
    per_window = width // step
    for j in range(nblk):
        window = q[:, (j // per_window) * width:(j // per_window + 1) * width]
        shift = (width - step * (j % per_window)) % width
        s3[j] = pltpu.roll(window, shift, 1) if shift else window
    over(nblk, b, lambda j: blk_copy(j, b).start())
    over(nsec, s, lambda j: sec_copy(j, s).wait_send())
    over(zc, z_hi, lambda zp: e_copy(zp, z_hi).wait_send())
    over(ng, g, lambda gp: g_copy(gp, g).wait_send())
    total = reduce(nblk, b, lambda j: blk_copy(j, j).wait_recv(), r3, s3[b])
    out_ref[...] = total[0:out_ref.shape[0], 0:out_ref.shape[1]] * factor
    over(nblk, b, lambda j: blk_copy(j, b).wait_send())


def shards(velocity, geometry, mass, snapshots, eigvecs, mode_order, elem_map):
    nsec = lax.axis_size("sec")
    nblk = lax.axis_size("blk")
    fields, comps, elems, pts = velocity.shape
    m_count = snapshots.shape[0]
    weights = jnp.asarray(point_weights()).reshape(1, pts)
    modes = eigvecs.shape[1]
    mats = kron_matrices()
    mo = mode_order.reshape(1, modes)
    small = list(mats) + [geometry, mass, weights, velocity, snapshots]
    per_sec = fields // nsec
    chunks = m_count // 128
    factor = 0.25 / math.sqrt(elems * nsec * nblk)
    kernel = functools.partial(comm_kernel, nsec, nblk, factor)
    tile = (nblk, per_sec, 128)
    vmem = pl.BlockSpec(memory_space=pltpu.VMEM)
    hbm = pl.BlockSpec(memory_space=pl.ANY)
    out = pl.pallas_call(
        kernel,
        out_shape=jax.ShapeDtypeStruct((per_sec, modes // nblk), F32),
        in_specs=[hbm] * 9 + [pl.BlockSpec(memory_space=pltpu.SMEM)] + [hbm] * 2,
        out_specs=vmem,
        scratch_shapes=[pltpu.VMEM(x.shape, x.dtype) for x in small + [eigvecs, mo]] + [
            pltpu.SemaphoreType.DMA((len(small) + 2,)),
            pltpu.VMEM((nsec, chunks * per_sec, 128), F32),
            pltpu.VMEM((nsec, chunks * per_sec, 128), F32),
            pltpu.VMEM((4,) + eigvecs.shape, F32),
            pltpu.VMEM((nblk // 4, per_sec, 128), F32),
            pltpu.VMEM((nblk // 4, per_sec, 128), F32),
            pltpu.VMEM(tile, F32),
            pltpu.VMEM(tile, F32),
            pltpu.VMEM((comps * elems * fields, 3 * pts), F32),
            pltpu.SemaphoreType.DMA((nsec,)),
            pltpu.SemaphoreType.DMA((nsec,)),
            pltpu.SemaphoreType.DMA((4,)),
            pltpu.SemaphoreType.DMA((4,)),
            pltpu.SemaphoreType.DMA((nblk // 4,)),
            pltpu.SemaphoreType.DMA((nblk // 4,)),
            pltpu.SemaphoreType.DMA((nblk,)),
            pltpu.SemaphoreType.DMA((nblk,)),
        ],
        compiler_params=pltpu.CompilerParams(
            collective_id=0, has_side_effects=True),
    )(velocity, *mats, geometry, mass, weights, snapshots, elem_map, eigvecs, mo)
    return out


def solution(mesh):
    placed = (
        P(None, None, ("sec", "blk"), None),
        P(None, ("sec", "blk"), None),
        P(("sec", "blk"), None),
        P(None, None, ("sec", "blk"), None),
        P("blk", None),
        P(),
        P(("sec", "blk")),
    )
    return jax.shard_map(
        shards, mesh=mesh, in_specs=placed, out_specs=P("sec", "blk"), check_vma=False
    )
```

```python
import functools
import math

import ml_dtypes

import jax
import jax.numpy as jnp
import numpy as np
from jax import lax
from jax.experimental import pallas as pl
from jax.experimental.pallas import tpu as pltpu
from jax.sharding import PartitionSpec as P

GLL_NODES = np.array(
    [
        -1.0,
        -0.8717401485096066,
        -0.5917001814331423,
        -0.2092992179024789,
        0.2092992179024789,
        0.5917001814331423,
        0.8717401485096066,
        1.0,
    ]
)
GLL_WEIGHTS = np.array(
    [
        1.0 / 28.0,
        0.2107042271435061,
        0.3411226924835044,
        0.4124587946587038,
        0.4124587946587038,
        0.3411226924835044,
        0.2107042271435061,
        1.0 / 28.0,
    ]
)


def legendre_seven(nodes):
    before = nodes * 0.0 + 1.0
    current = nodes * 1.0
    for order in range(1, 7):
        following = ((2.0 * order + 1.0) * nodes * current - order * before) / (order + 1.0)
        before = current
        current = following
    return current


def derivative_matrix():
    degree = 7
    values = legendre_seven(GLL_NODES)
    result = np.zeros((8, 8))
    for row_idx in range(8):
        for col_idx in range(8):
            if row_idx != col_idx:
                result[row_idx, col_idx] = values[row_idx] / (
                    values[col_idx] * (GLL_NODES[row_idx] - GLL_NODES[col_idx])
                )
    result[0, 0] = -degree * (degree + 1) / 4.0
    result[7, 7] = degree * (degree + 1) / 4.0
    return result.astype(np.float32)


def point_weights():
    cube = GLL_WEIGHTS[:, None, None] * GLL_WEIGHTS[None, :, None] * GLL_WEIGHTS[None, None, :]
    return cube.reshape(512).astype(np.float32)


MESH_IDS = pl.DeviceIdType.MESH
F32 = jnp.float32
BF16 = jnp.bfloat16


def host_split(full):
    upper = full.astype(ml_dtypes.bfloat16)
    lower = (full - upper.astype(np.float32)).astype(ml_dtypes.bfloat16)
    return jnp.asarray(upper), jnp.asarray(lower)


def kron_matrices():
    dt = derivative_matrix().astype(np.float64).T
    eye8 = np.eye(8)
    along_r = np.kron(dt, np.eye(64)).astype(np.float32)
    pair = np.eye(2)
    along_st = np.concatenate(
        [np.kron(pair, np.kron(dt, eye8)), np.kron(pair, np.kron(eye8, dt))], axis=1
    ).astype(np.float32)
    return host_split(along_r) + host_split(along_st)


def split_dot(a, b):
    a_hi = a.astype(BF16)
    a_lo = (a - a_hi.astype(F32)).astype(BF16)
    b_hi = b.astype(BF16)
    b_lo = (b - b_hi.astype(F32)).astype(BF16)
    out = jnp.dot(a_hi, b_hi, preferred_element_type=F32)
    out = out + jnp.dot(a_hi, b_lo, preferred_element_type=F32)
    return out + jnp.dot(a_lo, b_hi, preferred_element_type=F32)


def exact_select(a, onehot):
    hi = a.astype(BF16)
    rest = a - hi.astype(F32)
    mid = rest.astype(BF16)
    lo = (rest - mid.astype(F32)).astype(BF16)
    out = jnp.dot(hi, onehot, preferred_element_type=F32)
    out = out + jnp.dot(mid, onehot, preferred_element_type=F32)
    return out + jnp.dot(lo, onehot, preferred_element_type=F32)


def comm_kernel(nsec, nblk, factor, v_hbm, mr_hi_hbm, mr_lo_hbm, st_hi_hbm, st_lo_hbm, geo_hbm,
                mass_hbm, w_hbm, snap_hbm, em_ref, e_hbm, mo_hbm, out_ref,
                mr_hi, mr_lo, st_hi, st_lo, geo_ref, mass_ref, w_ref, v_ref, snap_ref, e_ref, mo_ref, lsem,
                cin, r1, eg, s2, r2, s3, r3, deriv, ss1, rs1, sse, rse, ss2, rs2, ss3, rs3):
    s = lax.axis_index("sec")
    b = lax.axis_index("blk")

    loads = [
        pltpu.make_async_copy(src, dst, lsem.at[i])
        for i, (src, dst) in enumerate((
            (mr_hi_hbm, mr_hi), (mr_lo_hbm, mr_lo), (st_hi_hbm, st_hi), (st_lo_hbm, st_lo),
            (geo_hbm, geo_ref), (mass_hbm, mass_ref), (w_hbm, w_ref), (v_hbm, v_ref),
            (snap_hbm, snap_ref), (e_hbm, e_ref), (mo_hbm, mo_ref)))
    ]
    for load in loads:
        load.start()

    barrier = pltpu.get_barrier_semaphore()

    def greet_sec(d, c):
        peer = lax.rem(s + d, nsec)
        pl.semaphore_signal(barrier, 1, device_id=(peer, b), device_id_type=MESH_IDS)
        return c

    def greet_blk(d, c):
        peer = lax.rem(b + d, nblk)
        pl.semaphore_signal(barrier, 1, device_id=(s, peer), device_id_type=MESH_IDS)
        return c

    lax.fori_loop(1, nsec, greet_sec, 0)
    lax.fori_loop(1, nblk, greet_blk, 0)

    fields, comps, elems, pts = v_ref.shape
    for load in loads[:4] + loads[7:8]:
        load.wait()
    v = jnp.concatenate([v_ref[:, c, e, :] for c in range(3) for e in range(mass_ref.shape[0])], axis=0)
    deriv[:, 0:pts] = (jnp.dot(v, mr_hi[...], preferred_element_type=F32)
                       + jnp.dot(v, mr_lo[...], preferred_element_type=F32))
    chunk = st_hi.shape[0]
    for c in range(pts // chunk):
        part = v[:, c * chunk:(c + 1) * chunk]
        both = (jnp.dot(part, st_hi[...], preferred_element_type=F32)
                + jnp.dot(part, st_lo[...], preferred_element_type=F32))
        deriv[:, pts + c * chunk:pts + (c + 1) * chunk] = both[:, 0:chunk]
        deriv[:, 2 * pts + c * chunk:2 * pts + (c + 1) * chunk] = both[:, chunk:2 * chunk]

    def along(a, c, e):
        row = (c * elems + e) * fields
        return deriv[row:row + fields, a * pts:(a + 1) * pts]

    for load in loads[4:7]:
        load.wait()
    weighted = []
    for e in range(elems):
        def geo(k):
            return geo_ref[k, e:e + 1, :]

        def gradient(c, coord):
            return (geo(coord) * along(0, c, e) + geo(3 + coord) * along(1, c, e)
                    + geo(6 + coord) * along(2, c, e))

        scale = mass_ref[e:e + 1, :] * w_ref[...]
        vort = [gradient(2, 1) - gradient(1, 2), gradient(0, 2) - gradient(2, 0),
                gradient(1, 0) - gradient(0, 1)]
        weighted.append([(scale * x).astype(BF16) for x in vort])

    loads[8].wait()
    local = jnp.zeros((fields, snap_ref.shape[0]), F32)
    for c in range(comps):
        for j in range(elems):
            stored = jnp.zeros_like(weighted[0][c])
            for e in range(elems):
                stored = jnp.where(em_ref[e] == j, weighted[e][c], stored)
            local = local + lax.dot_general(
                stored, snap_ref[:, c, j, :], (((1,), (1,)), ((), ())),
                preferred_element_type=F32)

    per_sec = fields // nsec
    lanes = 128
    chunks = local.shape[1] // lanes
    for j in range(nsec):
        for qq in range(chunks):
            cin[j, qq * per_sec:(qq + 1) * per_sec, :] = local[
                j * per_sec:(j + 1) * per_sec, qq * lanes:(qq + 1) * lanes]

    for load in loads[9:]:
        load.wait()
    pl.semaphore_wait(barrier, (nsec - 1) + (nblk - 1))

    zc = 4
    y = b // (2 * zc)
    z_hi = lax.rem(b // 2, zc)
    core = lax.rem(b, 2)
    g = y * 2 + core
    ng = nblk // zc

    def g_device(gp):
        return (gp // 2) * (2 * zc) + z_hi * 2 + lax.rem(gp, 2)

    def z_device(zp):
        return y * (2 * zc) + zp * 2 + core

    def sec_copy(j, dst):
        return pltpu.make_async_remote_copy(
            cin.at[j], r1.at[dst], ss1.at[j], rs1.at[dst],
            device_id=(j, b), device_id_type=MESH_IDS)

    def e_copy(zp, slot):
        return pltpu.make_async_remote_copy(
            e_ref, eg.at[slot], sse.at[zp], rse.at[slot],
            device_id=(s, z_device(zp)), device_id_type=MESH_IDS)

    def g_copy(gp, slot):
        return pltpu.make_async_remote_copy(
            s2.at[gp], r2.at[slot], ss2.at[gp], rs2.at[slot],
            device_id=(s, g_device(gp)), device_id_type=MESH_IDS)

    def blk_copy(j, slot):
        return pltpu.make_async_remote_copy(
            s3.at[j], r3.at[slot], ss3.at[j], rs3.at[slot],
            device_id=(s, j), device_id_type=MESH_IDS)

    def over(n, me, fn):
        def body(d, c):
            fn(lax.rem(me + d, n))
            return c
        lax.fori_loop(1, n, body, 0)

    def reduce(n, me, wait, recv, acc):
        def body(d, a):
            j = lax.rem(me + d, n)
            wait(j)
            return a + recv[j]
        return lax.fori_loop(1, n, body, acc)

    over(zc, z_hi, lambda zp: e_copy(zp, z_hi).start())
    over(nsec, s, lambda j: sec_copy(j, s).start())
    cb = reduce(nsec, s, lambda j: sec_copy(j, j).wait_recv(), r1, cin[s])

    modes = e_ref.shape[1]
    width = 128
    per_sec = s2.shape[1]
    m_total = (cb.shape[0] // per_sec) * width
    rows = m_total // nblk
    lane_group = lax.broadcasted_iota(jnp.int32, (per_sec, width), 1) // rows
    for gp in range(ng):
        packed = jnp.zeros((per_sec, width), F32)
        for zp in range(zc):
            block = (gp // 2) * (2 * zc) + zp * 2 + gp % 2
            qq = (block * rows) // width
            window = cb[qq * per_sec:(qq + 1) * per_sec, :]
            shift = (rows * zp - (block * rows - qq * width)) % width
            moved = pltpu.roll(window, shift, 1) if shift else window
            packed = jnp.where(lane_group == zp, moved, packed)
        s2[gp] = packed
    over(ng, g, lambda gp: g_copy(gp, g).start())

    eg[z_hi] = e_ref[...]
    over(zc, z_hi, lambda zp: e_copy(zp, zp).wait_recv())
    cp = reduce(ng, g, lambda gp: g_copy(gp, gp).wait_recv(), r2, s2[g])
    sel = (lax.broadcasted_iota(jnp.int32, (modes, modes), 0) == mo_ref[...]).astype(BF16)
    e_part = exact_select(eg[...].reshape(zc * e_ref.shape[0], modes), sel)
    q = split_dot(cp[:, 0:zc * rows], e_part)

    step = modes // nblk
    per_window = width // step
    for j in range(nblk):
        window = q[:, (j // per_window) * width:(j // per_window + 1) * width]
        shift = (width - step * (j % per_window)) % width
        s3[j] = pltpu.roll(window, shift, 1) if shift else window
    ny = nblk // (2 * zc)

    def ring(d, n):
        return min(d, n - d)

    offsets = sorted(
        ((dy, dz, dc) for dy in range(ny) for dz in range(zc) for dc in range(2)
         if (dy, dz, dc) != (0, 0, 0)),
        key=lambda o: -(4 * ring(o[1], zc) + ring(o[0], ny) + o[2]))
    for dy, dz, dc in offsets:
        peer = (lax.rem(y + dy, ny) * zc + lax.rem(z_hi + dz, zc)) * 2 + lax.rem(core + dc, 2)
        blk_copy(peer, b).start()
    over(nsec, s, lambda j: sec_copy(j, s).wait_send())
    over(zc, z_hi, lambda zp: e_copy(zp, z_hi).wait_send())
    over(ng, g, lambda gp: g_copy(gp, g).wait_send())
    total = reduce(nblk, b, lambda j: blk_copy(j, j).wait_recv(), r3, s3[b])
    out_ref[...] = total[0:out_ref.shape[0], 0:out_ref.shape[1]] * factor
    over(nblk, b, lambda j: blk_copy(j, b).wait_send())


def shards(velocity, geometry, mass, snapshots, eigvecs, mode_order, elem_map):
    nsec = lax.axis_size("sec")
    nblk = lax.axis_size("blk")
    fields, comps, elems, pts = velocity.shape
    m_count = snapshots.shape[0]
    weights = jnp.asarray(point_weights()).reshape(1, pts)
    modes = eigvecs.shape[1]
    mats = kron_matrices()
    mo = mode_order.reshape(1, modes)
    small = list(mats) + [geometry, mass, weights, velocity, snapshots]
    per_sec = fields // nsec
    chunks = m_count // 128
    factor = 0.25 / math.sqrt(elems * nsec * nblk)
    kernel = functools.partial(comm_kernel, nsec, nblk, factor)
    tile = (nblk, per_sec, 128)
    vmem = pl.BlockSpec(memory_space=pltpu.VMEM)
    hbm = pl.BlockSpec(memory_space=pl.ANY)
    out = pl.pallas_call(
        kernel,
        out_shape=jax.ShapeDtypeStruct((per_sec, modes // nblk), F32),
        in_specs=[hbm] * 9 + [pl.BlockSpec(memory_space=pltpu.SMEM)] + [hbm] * 2,
        out_specs=vmem,
        scratch_shapes=[pltpu.VMEM(x.shape, x.dtype) for x in small + [eigvecs, mo]] + [
            pltpu.SemaphoreType.DMA((len(small) + 2,)),
            pltpu.VMEM((nsec, chunks * per_sec, 128), F32),
            pltpu.VMEM((nsec, chunks * per_sec, 128), F32),
            pltpu.VMEM((4,) + eigvecs.shape, F32),
            pltpu.VMEM((nblk // 4, per_sec, 128), F32),
            pltpu.VMEM((nblk // 4, per_sec, 128), F32),
            pltpu.VMEM(tile, F32),
            pltpu.VMEM(tile, F32),
            pltpu.VMEM((comps * elems * fields, 3 * pts), F32),
            pltpu.SemaphoreType.DMA((nsec,)),
            pltpu.SemaphoreType.DMA((nsec,)),
            pltpu.SemaphoreType.DMA((4,)),
            pltpu.SemaphoreType.DMA((4,)),
            pltpu.SemaphoreType.DMA((nblk // 4,)),
            pltpu.SemaphoreType.DMA((nblk // 4,)),
            pltpu.SemaphoreType.DMA((nblk,)),
            pltpu.SemaphoreType.DMA((nblk,)),
        ],
        compiler_params=pltpu.CompilerParams(
            collective_id=0, has_side_effects=True),
    )(velocity, *mats, geometry, mass, weights, snapshots, elem_map, eigvecs, mo)
    return out


def solution(mesh):
    placed = (
        P(None, None, ("sec", "blk"), None),
        P(None, ("sec", "blk"), None),
        P(("sec", "blk"), None),
        P(None, None, ("sec", "blk"), None),
        P("blk", None),
        P(),
        P(("sec", "blk")),
    )
    return jax.shard_map(
        shards, mesh=mesh, in_specs=placed, out_specs=P("sec", "blk"), check_vma=False
    )
```

```python
import functools
import math

import ml_dtypes

import jax
import jax.numpy as jnp
import numpy as np
from jax import lax
from jax.experimental import pallas as pl
from jax.experimental.pallas import tpu as pltpu
from jax.sharding import PartitionSpec as P

GLL_NODES = np.array(
    [
        -1.0,
        -0.8717401485096066,
        -0.5917001814331423,
        -0.2092992179024789,
        0.2092992179024789,
        0.5917001814331423,
        0.8717401485096066,
        1.0,
    ]
)
GLL_WEIGHTS = np.array(
    [
        1.0 / 28.0,
        0.2107042271435061,
        0.3411226924835044,
        0.4124587946587038,
        0.4124587946587038,
        0.3411226924835044,
        0.2107042271435061,
        1.0 / 28.0,
    ]
)


def legendre_seven(nodes):
    before = nodes * 0.0 + 1.0
    current = nodes * 1.0
    for order in range(1, 7):
        following = ((2.0 * order + 1.0) * nodes * current - order * before) / (order + 1.0)
        before = current
        current = following
    return current


def derivative_matrix():
    degree = 7
    values = legendre_seven(GLL_NODES)
    result = np.zeros((8, 8))
    for row_idx in range(8):
        for col_idx in range(8):
            if row_idx != col_idx:
                result[row_idx, col_idx] = values[row_idx] / (
                    values[col_idx] * (GLL_NODES[row_idx] - GLL_NODES[col_idx])
                )
    result[0, 0] = -degree * (degree + 1) / 4.0
    result[7, 7] = degree * (degree + 1) / 4.0
    return result.astype(np.float32)


def point_weights():
    cube = GLL_WEIGHTS[:, None, None] * GLL_WEIGHTS[None, :, None] * GLL_WEIGHTS[None, None, :]
    return cube.reshape(512).astype(np.float32)


MESH_IDS = pl.DeviceIdType.MESH
F32 = jnp.float32
BF16 = jnp.bfloat16


def host_split(full):
    upper = full.astype(ml_dtypes.bfloat16)
    lower = (full - upper.astype(np.float32)).astype(ml_dtypes.bfloat16)
    return jnp.asarray(upper), jnp.asarray(lower)


def kron_matrices():
    dt = derivative_matrix().astype(np.float64).T
    eye8 = np.eye(8)
    along_r = np.kron(dt, np.eye(64)).astype(np.float32)
    pair = np.eye(2)
    along_st = np.concatenate(
        [np.kron(pair, np.kron(dt, eye8)), np.kron(pair, np.kron(eye8, dt))], axis=1
    ).astype(np.float32)
    return host_split(along_r) + host_split(along_st)


def split_dot(a, b):
    a_hi = a.astype(BF16)
    a_lo = (a - a_hi.astype(F32)).astype(BF16)
    b_hi = b.astype(BF16)
    b_lo = (b - b_hi.astype(F32)).astype(BF16)
    out = jnp.dot(a_hi, b_hi, preferred_element_type=F32)
    out = out + jnp.dot(a_hi, b_lo, preferred_element_type=F32)
    return out + jnp.dot(a_lo, b_hi, preferred_element_type=F32)


def exact_select(a, onehot):
    hi = a.astype(BF16)
    rest = a - hi.astype(F32)
    mid = rest.astype(BF16)
    lo = (rest - mid.astype(F32)).astype(BF16)
    out = jnp.dot(hi, onehot, preferred_element_type=F32)
    out = out + jnp.dot(mid, onehot, preferred_element_type=F32)
    return out + jnp.dot(lo, onehot, preferred_element_type=F32)


def comm_kernel(nsec, nblk, factor, v_hbm, mr_hi_hbm, mr_lo_hbm, st_hi_hbm, st_lo_hbm, geo_hbm,
                mass_hbm, w_hbm, snap_hbm, em_ref, e_hbm, mo_hbm, out_ref,
                mr_hi, mr_lo, st_hi, st_lo, geo_ref, mass_ref, w_ref, v_ref, snap_ref, e_ref, mo_ref, lsem, prod,
                cin, r1, eg, s2, r2, s3, r3, deriv, ss1, rs1, sse, rse, ss2, rs2, ss3, rs3):
    s = lax.axis_index("sec")
    b = lax.axis_index("blk")

    loads = [
        pltpu.make_async_copy(src, dst, lsem.at[i])
        for i, (src, dst) in enumerate((
            (mr_hi_hbm, mr_hi), (mr_lo_hbm, mr_lo), (st_hi_hbm, st_hi), (st_lo_hbm, st_lo),
            (geo_hbm, geo_ref), (mass_hbm, mass_ref), (w_hbm, w_ref), (v_hbm, v_ref),
            (snap_hbm, snap_ref), (e_hbm, e_ref), (mo_hbm, mo_ref)))
    ]
    for load in loads:
        load.start()

    barrier = pltpu.get_barrier_semaphore()

    def greet_sec(d, c):
        peer = lax.rem(s + d, nsec)
        pl.semaphore_signal(barrier, 1, device_id=(peer, b), device_id_type=MESH_IDS)
        return c

    def greet_blk(d, c):
        peer = lax.rem(b + d, nblk)
        pl.semaphore_signal(barrier, 1, device_id=(s, peer), device_id_type=MESH_IDS)
        return c

    lax.fori_loop(1, nsec, greet_sec, 0)
    lax.fori_loop(1, nblk, greet_blk, 0)

    fields, comps, elems, pts = v_ref.shape
    for load in loads[:4] + loads[7:8]:
        load.wait()
    v = jnp.concatenate([v_ref[:, c, e, :] for c in range(3) for e in range(mass_ref.shape[0])], axis=0)
    deriv[:, 0:pts] = (jnp.dot(v, mr_hi[...], preferred_element_type=F32)
                       + jnp.dot(v, mr_lo[...], preferred_element_type=F32))
    chunk = st_hi.shape[0]
    for c in range(pts // chunk):
        part = v[:, c * chunk:(c + 1) * chunk]
        both = (jnp.dot(part, st_hi[...], preferred_element_type=F32)
                + jnp.dot(part, st_lo[...], preferred_element_type=F32))
        deriv[:, pts + c * chunk:pts + (c + 1) * chunk] = both[:, 0:chunk]
        deriv[:, 2 * pts + c * chunk:2 * pts + (c + 1) * chunk] = both[:, chunk:2 * chunk]

    def along(a, c, e):
        row = (c * elems + e) * fields
        return deriv[row:row + fields, a * pts:(a + 1) * pts]

    for load in loads[4:7]:
        load.wait()
    weighted = []
    for e in range(elems):
        def geo(k):
            return geo_ref[k, e:e + 1, :]

        def gradient(c, coord):
            return (geo(coord) * along(0, c, e) + geo(3 + coord) * along(1, c, e)
                    + geo(6 + coord) * along(2, c, e))

        scale = mass_ref[e:e + 1, :] * w_ref[...]
        vort = [gradient(2, 1) - gradient(1, 2), gradient(0, 2) - gradient(2, 0),
                gradient(1, 0) - gradient(0, 1)]
        weighted.append([(scale * x).astype(BF16) for x in vort])

    loads[8].wait()
    m_count = snap_ref.shape[0]
    local_t = jnp.zeros((m_count, 2 * fields), F32)
    for c in range(comps):
        slots = []
        for j in range(elems):
            stored = jnp.zeros_like(weighted[0][c])
            for e in range(elems):
                stored = jnp.where(em_ref[e] == j, weighted[e][c], stored)
            slots.append(stored)
        pair = snap_ref[:, c, :, :].reshape(elems * m_count, pts)
        prod[...] = lax.dot_general(
            pair, jnp.concatenate(slots, axis=0), (((1,), (1,)), ((), ())),
            preferred_element_type=F32)
        even = prod[pl.ds(0, m_count, stride=2), :]
        odd = prod[pl.ds(1, m_count, stride=2), :]
        local_t = local_t + even + pltpu.roll(odd, fields, 1)
    local = local_t.T[0:fields, :]

    per_sec = fields // nsec
    lanes = 128
    chunks = local.shape[1] // lanes
    for j in range(nsec):
        for qq in range(chunks):
            cin[j, qq * per_sec:(qq + 1) * per_sec, :] = local[
                j * per_sec:(j + 1) * per_sec, qq * lanes:(qq + 1) * lanes]

    for load in loads[9:]:
        load.wait()
    pl.semaphore_wait(barrier, (nsec - 1) + (nblk - 1))

    zc = 4
    y = b // (2 * zc)
    z_hi = lax.rem(b // 2, zc)
    core = lax.rem(b, 2)
    g = y * 2 + core
    ng = nblk // zc

    def g_device(gp):
        return (gp // 2) * (2 * zc) + z_hi * 2 + lax.rem(gp, 2)

    def z_device(zp):
        return y * (2 * zc) + zp * 2 + core

    def sec_copy(j, dst):
        return pltpu.make_async_remote_copy(
            cin.at[j], r1.at[dst], ss1.at[j], rs1.at[dst],
            device_id=(j, b), device_id_type=MESH_IDS)

    def e_copy(zp, slot):
        return pltpu.make_async_remote_copy(
            e_ref, eg.at[slot], sse.at[zp], rse.at[slot],
            device_id=(s, z_device(zp)), device_id_type=MESH_IDS)

    def g_copy(gp, slot):
        return pltpu.make_async_remote_copy(
            s2.at[gp], r2.at[slot], ss2.at[gp], rs2.at[slot],
            device_id=(s, g_device(gp)), device_id_type=MESH_IDS)

    def blk_copy(j, slot):
        return pltpu.make_async_remote_copy(
            s3.at[j], r3.at[slot], ss3.at[j], rs3.at[slot],
            device_id=(s, j), device_id_type=MESH_IDS)

    def over(n, me, fn):
        def body(d, c):
            fn(lax.rem(me + d, n))
            return c
        lax.fori_loop(1, n, body, 0)

    def reduce(n, me, wait, recv, acc):
        def body(d, a):
            j = lax.rem(me + d, n)
            wait(j)
            return a + recv[j]
        return lax.fori_loop(1, n, body, acc)

    over(zc, z_hi, lambda zp: e_copy(zp, z_hi).start())
    over(nsec, s, lambda j: sec_copy(j, s).start())
    cb = reduce(nsec, s, lambda j: sec_copy(j, j).wait_recv(), r1, cin[s])

    modes = e_ref.shape[1]
    width = 128
    per_sec = s2.shape[1]
    m_total = (cb.shape[0] // per_sec) * width
    rows = m_total // nblk
    lane_group = lax.broadcasted_iota(jnp.int32, (per_sec, width), 1) // rows
    for gp in range(ng):
        packed = jnp.zeros((per_sec, width), F32)
        for zp in range(zc):
            block = (gp // 2) * (2 * zc) + zp * 2 + gp % 2
            qq = (block * rows) // width
            window = cb[qq * per_sec:(qq + 1) * per_sec, :]
            shift = (rows * zp - (block * rows - qq * width)) % width
            moved = pltpu.roll(window, shift, 1) if shift else window
            packed = jnp.where(lane_group == zp, moved, packed)
        s2[gp] = packed
    over(ng, g, lambda gp: g_copy(gp, g).start())

    eg[z_hi] = e_ref[...]
    over(zc, z_hi, lambda zp: e_copy(zp, zp).wait_recv())
    cp = reduce(ng, g, lambda gp: g_copy(gp, gp).wait_recv(), r2, s2[g])
    sel = (lax.broadcasted_iota(jnp.int32, (modes, modes), 0) == mo_ref[...]).astype(BF16)
    e_part = exact_select(eg[...].reshape(zc * e_ref.shape[0], modes), sel)
    q = split_dot(cp[:, 0:zc * rows], e_part)

    step = modes // nblk
    per_window = width // step
    for j in range(nblk):
        window = q[:, (j // per_window) * width:(j // per_window + 1) * width]
        shift = (width - step * (j % per_window)) % width
        s3[j] = pltpu.roll(window, shift, 1) if shift else window
    ny = nblk // (2 * zc)

    def ring(d, n):
        return min(d, n - d)

    offsets = sorted(
        ((dy, dz, dc) for dy in range(ny) for dz in range(zc) for dc in range(2)
         if (dy, dz, dc) != (0, 0, 0)),
        key=lambda o: -(4 * ring(o[1], zc) + ring(o[0], ny) + o[2]))
    for dy, dz, dc in offsets:
        peer = (lax.rem(y + dy, ny) * zc + lax.rem(z_hi + dz, zc)) * 2 + lax.rem(core + dc, 2)
        blk_copy(peer, b).start()
    over(nsec, s, lambda j: sec_copy(j, s).wait_send())
    over(zc, z_hi, lambda zp: e_copy(zp, z_hi).wait_send())
    over(ng, g, lambda gp: g_copy(gp, g).wait_send())
    total = reduce(nblk, b, lambda j: blk_copy(j, j).wait_recv(), r3, s3[b])
    out_ref[...] = total[0:out_ref.shape[0], 0:out_ref.shape[1]] * factor
    over(nblk, b, lambda j: blk_copy(j, b).wait_send())


def shards(velocity, geometry, mass, snapshots, eigvecs, mode_order, elem_map):
    nsec = lax.axis_size("sec")
    nblk = lax.axis_size("blk")
    fields, comps, elems, pts = velocity.shape
    m_count = snapshots.shape[0]
    weights = jnp.asarray(point_weights()).reshape(1, pts)
    modes = eigvecs.shape[1]
    mats = kron_matrices()
    mo = mode_order.reshape(1, modes)
    small = list(mats) + [geometry, mass, weights, velocity, snapshots]
    per_sec = fields // nsec
    chunks = m_count // 128
    factor = 0.25 / math.sqrt(elems * nsec * nblk)
    kernel = functools.partial(comm_kernel, nsec, nblk, factor)
    tile = (nblk, per_sec, 128)
    vmem = pl.BlockSpec(memory_space=pltpu.VMEM)
    hbm = pl.BlockSpec(memory_space=pl.ANY)
    out = pl.pallas_call(
        kernel,
        out_shape=jax.ShapeDtypeStruct((per_sec, modes // nblk), F32),
        in_specs=[hbm] * 9 + [pl.BlockSpec(memory_space=pltpu.SMEM)] + [hbm] * 2,
        out_specs=vmem,
        scratch_shapes=[pltpu.VMEM(x.shape, x.dtype) for x in small + [eigvecs, mo]] + [
            pltpu.SemaphoreType.DMA((len(small) + 2,)),
            pltpu.VMEM((2 * snapshots.shape[0], 2 * fields), F32),
            pltpu.VMEM((nsec, chunks * per_sec, 128), F32),
            pltpu.VMEM((nsec, chunks * per_sec, 128), F32),
            pltpu.VMEM((4,) + eigvecs.shape, F32),
            pltpu.VMEM((nblk // 4, per_sec, 128), F32),
            pltpu.VMEM((nblk // 4, per_sec, 128), F32),
            pltpu.VMEM(tile, F32),
            pltpu.VMEM(tile, F32),
            pltpu.VMEM((comps * elems * fields, 3 * pts), F32),
            pltpu.SemaphoreType.DMA((nsec,)),
            pltpu.SemaphoreType.DMA((nsec,)),
            pltpu.SemaphoreType.DMA((4,)),
            pltpu.SemaphoreType.DMA((4,)),
            pltpu.SemaphoreType.DMA((nblk // 4,)),
            pltpu.SemaphoreType.DMA((nblk // 4,)),
            pltpu.SemaphoreType.DMA((nblk,)),
            pltpu.SemaphoreType.DMA((nblk,)),
        ],
        compiler_params=pltpu.CompilerParams(
            collective_id=0, has_side_effects=True),
    )(velocity, *mats, geometry, mass, weights, snapshots, elem_map, eigvecs, mo)
    return out


def solution(mesh):
    placed = (
        P(None, None, ("sec", "blk"), None),
        P(None, ("sec", "blk"), None),
        P(("sec", "blk"), None),
        P(None, None, ("sec", "blk"), None),
        P("blk", None),
        P(),
        P(("sec", "blk")),
    )
    return jax.shard_map(
        shards, mesh=mesh, in_specs=placed, out_specs=P("sec", "blk"), check_vma=False
    )
```

```python
import functools
import math

import ml_dtypes

import jax
import jax.numpy as jnp
import numpy as np
from jax import lax
from jax.experimental import pallas as pl
from jax.experimental.pallas import tpu as pltpu
from jax.sharding import PartitionSpec as P

GLL_NODES = np.array(
    [
        -1.0,
        -0.8717401485096066,
        -0.5917001814331423,
        -0.2092992179024789,
        0.2092992179024789,
        0.5917001814331423,
        0.8717401485096066,
        1.0,
    ]
)
GLL_WEIGHTS = np.array(
    [
        1.0 / 28.0,
        0.2107042271435061,
        0.3411226924835044,
        0.4124587946587038,
        0.4124587946587038,
        0.3411226924835044,
        0.2107042271435061,
        1.0 / 28.0,
    ]
)


def legendre_seven(nodes):
    before = nodes * 0.0 + 1.0
    current = nodes * 1.0
    for order in range(1, 7):
        following = ((2.0 * order + 1.0) * nodes * current - order * before) / (order + 1.0)
        before = current
        current = following
    return current


def derivative_matrix():
    degree = 7
    values = legendre_seven(GLL_NODES)
    result = np.zeros((8, 8))
    for row_idx in range(8):
        for col_idx in range(8):
            if row_idx != col_idx:
                result[row_idx, col_idx] = values[row_idx] / (
                    values[col_idx] * (GLL_NODES[row_idx] - GLL_NODES[col_idx])
                )
    result[0, 0] = -degree * (degree + 1) / 4.0
    result[7, 7] = degree * (degree + 1) / 4.0
    return result.astype(np.float32)


def point_weights():
    cube = GLL_WEIGHTS[:, None, None] * GLL_WEIGHTS[None, :, None] * GLL_WEIGHTS[None, None, :]
    return cube.reshape(512).astype(np.float32)


MESH_IDS = pl.DeviceIdType.MESH
F32 = jnp.float32
BF16 = jnp.bfloat16


def host_split(full):
    upper = full.astype(ml_dtypes.bfloat16)
    lower = (full - upper.astype(np.float32)).astype(ml_dtypes.bfloat16)
    return jnp.asarray(upper), jnp.asarray(lower)


def kron_matrices():
    dt = derivative_matrix().astype(np.float64).T
    eye8 = np.eye(8)
    along_r = np.kron(dt, np.eye(64)).astype(np.float32)
    pair = np.eye(2)
    along_st = np.concatenate(
        [np.kron(pair, np.kron(dt, eye8)), np.kron(pair, np.kron(eye8, dt))], axis=1
    ).astype(np.float32)
    return host_split(along_r) + host_split(along_st)


def split_dot(a, b):
    a_hi = a.astype(BF16)
    a_lo = (a - a_hi.astype(F32)).astype(BF16)
    b_hi = b.astype(BF16)
    b_lo = (b - b_hi.astype(F32)).astype(BF16)
    out = jnp.dot(a_hi, b_hi, preferred_element_type=F32)
    out = out + jnp.dot(a_hi, b_lo, preferred_element_type=F32)
    return out + jnp.dot(a_lo, b_hi, preferred_element_type=F32)


def exact_select(a, onehot):
    hi = a.astype(BF16)
    rest = a - hi.astype(F32)
    mid = rest.astype(BF16)
    lo = (rest - mid.astype(F32)).astype(BF16)
    out = jnp.dot(hi, onehot, preferred_element_type=F32)
    out = out + jnp.dot(mid, onehot, preferred_element_type=F32)
    return out + jnp.dot(lo, onehot, preferred_element_type=F32)


def comm_kernel(nsec, nblk, factor, v_hbm, mr_hi_hbm, mr_lo_hbm, st_hi_hbm, st_lo_hbm, geo_hbm,
                mass_hbm, w_hbm, snap_hbm, em_ref, e_hbm, mo_hbm, out_ref,
                mr_hi, mr_lo, st_hi, st_lo, geo_ref, mass_ref, w_ref, v_ref, snap_ref, e_ref, mo_ref, lsem, prod,
                cin, r1, eg, s2, r2, s3, r3, deriv, ss1, rs1, sse, rse, ss2, rs2, ss3, rs3):
    s = lax.axis_index("sec")
    b = lax.axis_index("blk")

    loads = [
        pltpu.make_async_copy(src, dst, lsem.at[i])
        for i, (src, dst) in enumerate((
            (mr_hi_hbm, mr_hi), (mr_lo_hbm, mr_lo), (st_hi_hbm, st_hi), (st_lo_hbm, st_lo),
            (geo_hbm, geo_ref), (mass_hbm, mass_ref), (w_hbm, w_ref), (v_hbm, v_ref),
            (snap_hbm, snap_ref), (e_hbm, e_ref), (mo_hbm, mo_ref)))
    ]
    for load in loads:
        load.start()

    barrier = pltpu.get_barrier_semaphore()

    def greet_sec(d, c):
        peer = lax.rem(s + d, nsec)
        pl.semaphore_signal(barrier, 1, device_id=(peer, b), device_id_type=MESH_IDS)
        return c

    def greet_blk(d, c):
        peer = lax.rem(b + d, nblk)
        pl.semaphore_signal(barrier, 1, device_id=(s, peer), device_id_type=MESH_IDS)
        return c

    lax.fori_loop(1, nsec, greet_sec, 0)
    lax.fori_loop(1, nblk, greet_blk, 0)

    fields, comps, elems, pts = v_ref.shape
    for load in loads[:4] + loads[7:8]:
        load.wait()
    v = jnp.concatenate([v_ref[:, c, e, :] for c in range(3) for e in range(mass_ref.shape[0])], axis=0)
    deriv[:, 0:pts] = (jnp.dot(v, mr_hi[...], preferred_element_type=F32)
                       + jnp.dot(v, mr_lo[...], preferred_element_type=F32))
    chunk = st_hi.shape[0]
    for c in range(pts // chunk):
        part = v[:, c * chunk:(c + 1) * chunk]
        both = (jnp.dot(part, st_hi[...], preferred_element_type=F32)
                + jnp.dot(part, st_lo[...], preferred_element_type=F32))
        deriv[:, pts + c * chunk:pts + (c + 1) * chunk] = both[:, 0:chunk]
        deriv[:, 2 * pts + c * chunk:2 * pts + (c + 1) * chunk] = both[:, chunk:2 * chunk]

    def along(a, c, e):
        row = (c * elems + e) * fields
        return deriv[row:row + fields, a * pts:(a + 1) * pts]

    for load in loads[4:7]:
        load.wait()
    weighted = []
    for e in range(elems):
        def geo(k):
            return geo_ref[k, e:e + 1, :]

        def gradient(c, coord):
            return (geo(coord) * along(0, c, e) + geo(3 + coord) * along(1, c, e)
                    + geo(6 + coord) * along(2, c, e))

        scale = mass_ref[e:e + 1, :] * w_ref[...]
        vort = [gradient(2, 1) - gradient(1, 2), gradient(0, 2) - gradient(2, 0),
                gradient(1, 0) - gradient(0, 1)]
        weighted.append([(scale * x).astype(BF16) for x in vort])

    loads[8].wait()
    m_count = snap_ref.shape[0]
    local_t = jnp.zeros((m_count, 2 * fields), F32)
    for c in range(comps):
        slots = []
        for j in range(elems):
            stored = jnp.zeros_like(weighted[0][c])
            for e in range(elems):
                stored = jnp.where(em_ref[e] == j, weighted[e][c], stored)
            slots.append(stored)
        pair = snap_ref[:, c, :, :].reshape(elems * m_count, pts)
        prod[...] = lax.dot_general(
            pair, jnp.concatenate(slots, axis=0), (((1,), (1,)), ((), ())),
            preferred_element_type=F32)
        even = prod[pl.ds(0, m_count, stride=2), :]
        odd = prod[pl.ds(1, m_count, stride=2), :]
        local_t = local_t + even + pltpu.roll(odd, fields, 1)
    local = local_t.T[0:fields, :]

    per_sec = fields // nsec
    lanes = 128
    chunks = local.shape[1] // lanes
    for j in range(nsec):
        for qq in range(chunks):
            cin[j, qq * per_sec:(qq + 1) * per_sec, :] = local[
                j * per_sec:(j + 1) * per_sec, qq * lanes:(qq + 1) * lanes]

    for load in loads[9:]:
        load.wait()
    pl.semaphore_wait(barrier, (nsec - 1) + (nblk - 1))

    zc = 4
    y = b // (2 * zc)
    z_hi = lax.rem(b // 2, zc)
    core = lax.rem(b, 2)
    g = y * 2 + core
    ng = nblk // zc

    def g_device(gp):
        return (gp // 2) * (2 * zc) + z_hi * 2 + lax.rem(gp, 2)

    def z_device(zp):
        return y * (2 * zc) + zp * 2 + core

    def sec_copy(j, dst):
        return pltpu.make_async_remote_copy(
            cin.at[j], r1.at[dst], ss1.at[j], rs1.at[dst],
            device_id=(j, b), device_id_type=MESH_IDS)

    def e_copy(zp, slot):
        return pltpu.make_async_remote_copy(
            e_ref, eg.at[slot], sse.at[zp], rse.at[slot],
            device_id=(s, z_device(zp)), device_id_type=MESH_IDS)

    def g_copy(gp, slot):
        return pltpu.make_async_remote_copy(
            s2.at[gp], r2.at[slot], ss2.at[gp], rs2.at[slot],
            device_id=(s, g_device(gp)), device_id_type=MESH_IDS)

    def blk_copy(j, slot):
        return pltpu.make_async_remote_copy(
            s3.at[j], r3.at[slot], ss3.at[j], rs3.at[slot],
            device_id=(s, j), device_id_type=MESH_IDS)

    def over(n, me, fn):
        def body(d, c):
            fn(lax.rem(me + d, n))
            return c
        lax.fori_loop(1, n, body, 0)

    def reduce(n, me, wait, recv, acc):
        def body(d, a):
            j = lax.rem(me + d, n)
            wait(j)
            return a + recv[j]
        return lax.fori_loop(1, n, body, acc)

    over(zc, z_hi, lambda zp: e_copy(zp, z_hi).start())
    over(nsec, s, lambda j: sec_copy(j, s).start())
    cb = reduce(nsec, s, lambda j: sec_copy(j, j).wait_recv(), r1, cin[s])

    modes = e_ref.shape[1]
    width = 128
    per_sec = s2.shape[1]
    m_total = (cb.shape[0] // per_sec) * width
    rows = m_total // nblk
    lane_group = lax.broadcasted_iota(jnp.int32, (per_sec, width), 1) // rows
    for gp in range(ng):
        packed = jnp.zeros((per_sec, width), F32)
        for zp in range(zc):
            block = (gp // 2) * (2 * zc) + zp * 2 + gp % 2
            qq = (block * rows) // width
            window = cb[qq * per_sec:(qq + 1) * per_sec, :]
            shift = (rows * zp - (block * rows - qq * width)) % width
            moved = pltpu.roll(window, shift, 1) if shift else window
            packed = jnp.where(lane_group == zp, moved, packed)
        s2[gp] = packed
    over(ng, g, lambda gp: g_copy(gp, g).start())

    eg[z_hi] = e_ref[...]
    over(zc, z_hi, lambda zp: e_copy(zp, zp).wait_recv())
    cp = reduce(ng, g, lambda gp: g_copy(gp, gp).wait_recv(), r2, s2[g])
    sel = (lax.broadcasted_iota(jnp.int32, (modes, modes), 0) == mo_ref[...]).astype(BF16)
    e_part = exact_select(eg[...].reshape(zc * e_ref.shape[0], modes), sel)
    q = split_dot(cp[:, 0:zc * rows], e_part)

    step = modes // nblk
    per_window = width // step
    for j in range(nblk):
        window = q[:, (j // per_window) * width:(j // per_window + 1) * width]
        shift = (width - step * (j % per_window)) % width
        s3[j] = pltpu.roll(window, shift, 1) if shift else window
    ny = nblk // (2 * zc)

    def ring(d, n):
        return min(d, n - d)

    offsets = sorted(
        ((dy, dz, dc) for dy in range(ny) for dz in range(zc) for dc in range(2)
         if (dy, dz, dc) != (0, 0, 0)),
        key=lambda o: -(4 * ring(o[1], zc) + ring(o[0], ny) + o[2]))
    for dy, dz, dc in offsets:
        peer = (lax.rem(y + dy, ny) * zc + lax.rem(z_hi + dz, zc)) * 2 + lax.rem(core + dc, 2)
        blk_copy(peer, b).start()
    over(nsec, s, lambda j: sec_copy(j, s).wait_send())
    over(zc, z_hi, lambda zp: e_copy(zp, z_hi).wait_send())
    over(ng, g, lambda gp: g_copy(gp, g).wait_send())
    total = reduce(nblk, b, lambda j: blk_copy(j, j).wait_recv(), r3, s3[b])
    out_ref[...] = total[0:out_ref.shape[0], 0:out_ref.shape[1]]
    over(nblk, b, lambda j: blk_copy(j, b).wait_send())


def shards(velocity, geometry, mass, snapshots, eigvecs, mode_order, elem_map):
    nsec = lax.axis_size("sec")
    nblk = lax.axis_size("blk")
    fields, comps, elems, pts = velocity.shape
    m_count = snapshots.shape[0]
    weights = jnp.asarray(point_weights()).reshape(1, pts)
    modes = eigvecs.shape[1]
    mats = kron_matrices()
    mo = mode_order.reshape(1, modes)
    small = list(mats) + [geometry, mass, weights, velocity, snapshots]
    per_sec = fields // nsec
    chunks = m_count // 128
    factor = 0.25 / math.sqrt(elems * nsec * nblk)
    kernel = functools.partial(comm_kernel, nsec, nblk, factor)
    tile = (nblk, per_sec, 128)
    vmem = pl.BlockSpec(memory_space=pltpu.VMEM)
    hbm = pl.BlockSpec(memory_space=pl.ANY)
    out = pl.pallas_call(
        kernel,
        out_shape=jax.ShapeDtypeStruct((per_sec, modes // nblk), F32),
        in_specs=[hbm] * 9 + [pl.BlockSpec(memory_space=pltpu.SMEM)] + [hbm] * 2,
        out_specs=vmem,
        scratch_shapes=[pltpu.VMEM(x.shape, x.dtype) for x in small + [eigvecs, mo]] + [
            pltpu.SemaphoreType.DMA((len(small) + 2,)),
            pltpu.VMEM((2 * snapshots.shape[0], 2 * fields), F32),
            pltpu.VMEM((nsec, chunks * per_sec, 128), F32),
            pltpu.VMEM((nsec, chunks * per_sec, 128), F32),
            pltpu.VMEM((4,) + eigvecs.shape, F32),
            pltpu.VMEM((nblk // 4, per_sec, 128), F32),
            pltpu.VMEM((nblk // 4, per_sec, 128), F32),
            pltpu.VMEM(tile, F32),
            pltpu.VMEM(tile, F32),
            pltpu.VMEM((comps * elems * fields, 3 * pts), F32),
            pltpu.SemaphoreType.DMA((nsec,)),
            pltpu.SemaphoreType.DMA((nsec,)),
            pltpu.SemaphoreType.DMA((4,)),
            pltpu.SemaphoreType.DMA((4,)),
            pltpu.SemaphoreType.DMA((nblk // 4,)),
            pltpu.SemaphoreType.DMA((nblk // 4,)),
            pltpu.SemaphoreType.DMA((nblk,)),
            pltpu.SemaphoreType.DMA((nblk,)),
        ],
        compiler_params=pltpu.CompilerParams(
            collective_id=0, has_side_effects=True),
    )(velocity, *mats, geometry, mass, weights, snapshots, elem_map, eigvecs, mo)
    return out * factor


def solution(mesh):
    placed = (
        P(None, None, ("sec", "blk"), None),
        P(None, ("sec", "blk"), None),
        P(("sec", "blk"), None),
        P(None, None, ("sec", "blk"), None),
        P("blk", None),
        P(),
        P(("sec", "blk")),
    )
    return jax.shard_map(
        shards, mesh=mesh, in_specs=placed, out_specs=P("sec", "blk"), check_vma=False
    )
```

```python
import functools
import math

import ml_dtypes

import jax
import jax.numpy as jnp
import numpy as np
from jax import lax
from jax.experimental import pallas as pl
from jax.experimental.pallas import tpu as pltpu
from jax.sharding import PartitionSpec as P

GLL_NODES = np.array(
    [
        -1.0,
        -0.8717401485096066,
        -0.5917001814331423,
        -0.2092992179024789,
        0.2092992179024789,
        0.5917001814331423,
        0.8717401485096066,
        1.0,
    ]
)
GLL_WEIGHTS = np.array(
    [
        1.0 / 28.0,
        0.2107042271435061,
        0.3411226924835044,
        0.4124587946587038,
        0.4124587946587038,
        0.3411226924835044,
        0.2107042271435061,
        1.0 / 28.0,
    ]
)


def legendre_seven(nodes):
    before = nodes * 0.0 + 1.0
    current = nodes * 1.0
    for order in range(1, 7):
        following = ((2.0 * order + 1.0) * nodes * current - order * before) / (order + 1.0)
        before = current
        current = following
    return current


def derivative_matrix():
    degree = 7
    values = legendre_seven(GLL_NODES)
    result = np.zeros((8, 8))
    for row_idx in range(8):
        for col_idx in range(8):
            if row_idx != col_idx:
                result[row_idx, col_idx] = values[row_idx] / (
                    values[col_idx] * (GLL_NODES[row_idx] - GLL_NODES[col_idx])
                )
    result[0, 0] = -degree * (degree + 1) / 4.0
    result[7, 7] = degree * (degree + 1) / 4.0
    return result.astype(np.float32)


def point_weights():
    cube = GLL_WEIGHTS[:, None, None] * GLL_WEIGHTS[None, :, None] * GLL_WEIGHTS[None, None, :]
    return cube.reshape(512).astype(np.float32)


MESH_IDS = pl.DeviceIdType.MESH
F32 = jnp.float32
BF16 = jnp.bfloat16


def host_split(full):
    upper = full.astype(ml_dtypes.bfloat16)
    lower = (full - upper.astype(np.float32)).astype(ml_dtypes.bfloat16)
    return jnp.asarray(upper), jnp.asarray(lower)


def kron_matrices():
    dt = derivative_matrix().astype(np.float64).T
    eye8 = np.eye(8)
    along_r = np.kron(dt, np.eye(64)).astype(np.float32)
    pair = np.eye(2)
    along_st = np.concatenate(
        [np.kron(pair, np.kron(dt, eye8)), np.kron(pair, np.kron(eye8, dt))], axis=1
    ).astype(np.float32)
    return host_split(along_r) + host_split(along_st)


def split_dot(a, b):
    a_hi = a.astype(BF16)
    a_lo = (a - a_hi.astype(F32)).astype(BF16)
    b_hi = b.astype(BF16)
    b_lo = (b - b_hi.astype(F32)).astype(BF16)
    out = jnp.dot(a_hi, b_hi, preferred_element_type=F32)
    out = out + jnp.dot(a_hi, b_lo, preferred_element_type=F32)
    return out + jnp.dot(a_lo, b_hi, preferred_element_type=F32)


def exact_select(a, onehot):
    hi = a.astype(BF16)
    rest = a - hi.astype(F32)
    mid = rest.astype(BF16)
    lo = (rest - mid.astype(F32)).astype(BF16)
    out = jnp.dot(hi, onehot, preferred_element_type=F32)
    out = out + jnp.dot(mid, onehot, preferred_element_type=F32)
    return out + jnp.dot(lo, onehot, preferred_element_type=F32)


def comm_kernel(nsec, nblk, factor, v_hbm, mr_hi_hbm, mr_lo_hbm, st_hi_hbm, st_lo_hbm, geo_hbm,
                mass_hbm, w_hbm, snap_hbm, em_ref, e_hbm, mo_hbm, out_ref,
                mr_hi, mr_lo, st_hi, st_lo, geo_ref, mass_ref, w_ref, v_ref, snap_ref, e_ref, mo_ref, lsem, prod,
                cin, r1, eg, s2, r2, s3, r3, deriv, ss1, rs1, sse, rse, ss2, rs2, ss3, rs3):
    s = lax.axis_index("sec")
    b = lax.axis_index("blk")

    loads = [
        pltpu.make_async_copy(src, dst, lsem.at[i])
        for i, (src, dst) in enumerate((
            (mr_hi_hbm, mr_hi), (mr_lo_hbm, mr_lo), (st_hi_hbm, st_hi), (st_lo_hbm, st_lo),
            (geo_hbm, geo_ref), (mass_hbm, mass_ref), (w_hbm, w_ref), (v_hbm, v_ref),
            (snap_hbm, snap_ref), (e_hbm, e_ref), (mo_hbm, mo_ref)))
    ]
    for load in loads:
        load.start()

    barrier = pltpu.get_barrier_semaphore()

    def greet_sec(d, c):
        peer = lax.rem(s + d, nsec)
        pl.semaphore_signal(barrier, 1, device_id=(peer, b), device_id_type=MESH_IDS)
        return c

    def greet_blk(d, c):
        peer = lax.rem(b + d, nblk)
        pl.semaphore_signal(barrier, 1, device_id=(s, peer), device_id_type=MESH_IDS)
        return c

    zc = 4
    ny = nblk // (2 * zc)
    y = b // (2 * zc)
    z_hi = lax.rem(b // 2, zc)
    core = lax.rem(b, 2)
    nx = nsec // zc
    x = s // zc
    z_lo = lax.rem(s, zc)

    def ring(d, n):
        return min(d, n - d)

    far_blk = sorted(
        ((dy, dz, dc) for dy in range(ny) for dz in range(zc) for dc in range(2)
         if (dy, dz, dc) != (0, 0, 0)),
        key=lambda o: -(4 * ring(o[1], zc) + ring(o[0], ny) + o[2]))
    far_sec = sorted(
        ((dx, dl) for dx in range(nx) for dl in range(zc) if (dx, dl) != (0, 0)),
        key=lambda o: -ring(o[0], nx))

    def blk_peer(o):
        dy, dz, dc = o
        return (lax.rem(y + dy, ny) * zc + lax.rem(z_hi + dz, zc)) * 2 + lax.rem(core + dc, 2)

    def sec_peer(o):
        dx, dl = o
        return lax.rem(x + dx, nx) * zc + lax.rem(z_lo + dl, zc)

    for o in far_blk:
        pl.semaphore_signal(barrier, 1, device_id=(s, blk_peer(o)), device_id_type=MESH_IDS)
    for o in far_sec:
        pl.semaphore_signal(barrier, 1, device_id=(sec_peer(o), b), device_id_type=MESH_IDS)

    fields, comps, elems, pts = v_ref.shape
    for load in loads[:4] + loads[7:8]:
        load.wait()
    v = jnp.concatenate([v_ref[:, c, e, :] for c in range(3) for e in range(mass_ref.shape[0])], axis=0)
    deriv[:, 0:pts] = (jnp.dot(v, mr_hi[...], preferred_element_type=F32)
                       + jnp.dot(v, mr_lo[...], preferred_element_type=F32))
    chunk = st_hi.shape[0]
    for c in range(pts // chunk):
        part = v[:, c * chunk:(c + 1) * chunk]
        both = (jnp.dot(part, st_hi[...], preferred_element_type=F32)
                + jnp.dot(part, st_lo[...], preferred_element_type=F32))
        deriv[:, pts + c * chunk:pts + (c + 1) * chunk] = both[:, 0:chunk]
        deriv[:, 2 * pts + c * chunk:2 * pts + (c + 1) * chunk] = both[:, chunk:2 * chunk]

    def along(a, c, e):
        row = (c * elems + e) * fields
        return deriv[row:row + fields, a * pts:(a + 1) * pts]

    for load in loads[4:7]:
        load.wait()
    weighted = []
    for e in range(elems):
        def geo(k):
            return geo_ref[k, e:e + 1, :]

        def gradient(c, coord):
            return (geo(coord) * along(0, c, e) + geo(3 + coord) * along(1, c, e)
                    + geo(6 + coord) * along(2, c, e))

        scale = mass_ref[e:e + 1, :] * w_ref[...]
        vort = [gradient(2, 1) - gradient(1, 2), gradient(0, 2) - gradient(2, 0),
                gradient(1, 0) - gradient(0, 1)]
        weighted.append([(scale * x).astype(BF16) for x in vort])

    loads[8].wait()
    m_count = snap_ref.shape[0]
    local_t = jnp.zeros((m_count, 2 * fields), F32)
    for c in range(comps):
        slots = []
        for j in range(elems):
            stored = jnp.zeros_like(weighted[0][c])
            for e in range(elems):
                stored = jnp.where(em_ref[e] == j, weighted[e][c], stored)
            slots.append(stored)
        pair = snap_ref[:, c, :, :].reshape(elems * m_count, pts)
        prod[...] = lax.dot_general(
            pair, jnp.concatenate(slots, axis=0), (((1,), (1,)), ((), ())),
            preferred_element_type=F32)
        even = prod[pl.ds(0, m_count, stride=2), :]
        odd = prod[pl.ds(1, m_count, stride=2), :]
        local_t = local_t + even + pltpu.roll(odd, fields, 1)
    local = local_t.T[0:fields, :]

    per_sec = fields // nsec
    lanes = 128
    chunks = local.shape[1] // lanes
    for j in range(nsec):
        for qq in range(chunks):
            cin[j, qq * per_sec:(qq + 1) * per_sec, :] = local[
                j * per_sec:(j + 1) * per_sec, qq * lanes:(qq + 1) * lanes]

    for load in loads[9:]:
        load.wait()
    pl.semaphore_wait(barrier, (nsec - 1) + (nblk - 1))

    g = y * 2 + core
    ng = nblk // zc

    def g_device(gp):
        return (gp // 2) * (2 * zc) + z_hi * 2 + lax.rem(gp, 2)

    def z_device(zp):
        return y * (2 * zc) + zp * 2 + core

    def sec_copy(j, dst):
        return pltpu.make_async_remote_copy(
            cin.at[j], r1.at[dst], ss1.at[j], rs1.at[dst],
            device_id=(j, b), device_id_type=MESH_IDS)

    def e_copy(zp, slot):
        return pltpu.make_async_remote_copy(
            e_ref, eg.at[slot], sse.at[zp], rse.at[slot],
            device_id=(s, z_device(zp)), device_id_type=MESH_IDS)

    def g_copy(gp, slot):
        return pltpu.make_async_remote_copy(
            s2.at[gp], r2.at[slot], ss2.at[gp], rs2.at[slot],
            device_id=(s, g_device(gp)), device_id_type=MESH_IDS)

    def blk_copy(j, slot):
        return pltpu.make_async_remote_copy(
            s3.at[j], r3.at[slot], ss3.at[j], rs3.at[slot],
            device_id=(s, j), device_id_type=MESH_IDS)

    def over(n, me, fn):
        def body(d, c):
            fn(lax.rem(me + d, n))
            return c
        lax.fori_loop(1, n, body, 0)

    def reduce(n, me, wait, recv, acc):
        def body(d, a):
            j = lax.rem(me + d, n)
            wait(j)
            return a + recv[j]
        return lax.fori_loop(1, n, body, acc)

    over(zc, z_hi, lambda zp: e_copy(zp, z_hi).start())
    for o in far_sec:
        sec_copy(sec_peer(o), s).start()
    cb = reduce(nsec, s, lambda j: sec_copy(j, j).wait_recv(), r1, cin[s])

    modes = e_ref.shape[1]
    width = 128
    per_sec = s2.shape[1]
    m_total = (cb.shape[0] // per_sec) * width
    rows = m_total // nblk
    lane_group = lax.broadcasted_iota(jnp.int32, (per_sec, width), 1) // rows
    for gp in range(ng):
        packed = jnp.zeros((per_sec, width), F32)
        for zp in range(zc):
            block = (gp // 2) * (2 * zc) + zp * 2 + gp % 2
            qq = (block * rows) // width
            window = cb[qq * per_sec:(qq + 1) * per_sec, :]
            shift = (rows * zp - (block * rows - qq * width)) % width
            moved = pltpu.roll(window, shift, 1) if shift else window
            packed = jnp.where(lane_group == zp, moved, packed)
        s2[gp] = packed
    over(ng, g, lambda gp: g_copy(gp, g).start())

    eg[z_hi] = e_ref[...]
    over(zc, z_hi, lambda zp: e_copy(zp, zp).wait_recv())
    cp = reduce(ng, g, lambda gp: g_copy(gp, gp).wait_recv(), r2, s2[g])
    sel = (lax.broadcasted_iota(jnp.int32, (modes, modes), 0) == mo_ref[...]).astype(BF16)
    e_part = exact_select(eg[...].reshape(zc * e_ref.shape[0], modes), sel)
    q = split_dot(cp[:, 0:zc * rows], e_part)

    step = modes // nblk
    per_window = width // step
    for j in range(nblk):
        window = q[:, (j // per_window) * width:(j // per_window + 1) * width]
        shift = (width - step * (j % per_window)) % width
        s3[j] = pltpu.roll(window, shift, 1) if shift else window
    for o in far_blk:
        blk_copy(blk_peer(o), b).start()
    over(nsec, s, lambda j: sec_copy(j, s).wait_send())
    over(zc, z_hi, lambda zp: e_copy(zp, z_hi).wait_send())
    over(ng, g, lambda gp: g_copy(gp, g).wait_send())
    total = reduce(nblk, b, lambda j: blk_copy(j, j).wait_recv(), r3, s3[b])
    out_ref[...] = total[0:out_ref.shape[0], 0:out_ref.shape[1]]
    over(nblk, b, lambda j: blk_copy(j, b).wait_send())


def shards(velocity, geometry, mass, snapshots, eigvecs, mode_order, elem_map):
    nsec = lax.axis_size("sec")
    nblk = lax.axis_size("blk")
    fields, comps, elems, pts = velocity.shape
    m_count = snapshots.shape[0]
    weights = jnp.asarray(point_weights()).reshape(1, pts)
    modes = eigvecs.shape[1]
    mats = kron_matrices()
    mo = mode_order.reshape(1, modes)
    small = list(mats) + [geometry, mass, weights, velocity, snapshots]
    per_sec = fields // nsec
    chunks = m_count // 128
    factor = 0.25 / math.sqrt(elems * nsec * nblk)
    kernel = functools.partial(comm_kernel, nsec, nblk, factor)
    tile = (nblk, per_sec, 128)
    vmem = pl.BlockSpec(memory_space=pltpu.VMEM)
    hbm = pl.BlockSpec(memory_space=pl.ANY)
    out = pl.pallas_call(
        kernel,
        out_shape=jax.ShapeDtypeStruct((per_sec, modes // nblk), F32),
        in_specs=[hbm] * 9 + [pl.BlockSpec(memory_space=pltpu.SMEM)] + [hbm] * 2,
        out_specs=vmem,
        scratch_shapes=[pltpu.VMEM(x.shape, x.dtype) for x in small + [eigvecs, mo]] + [
            pltpu.SemaphoreType.DMA((len(small) + 2,)),
            pltpu.VMEM((2 * snapshots.shape[0], 2 * fields), F32),
            pltpu.VMEM((nsec, chunks * per_sec, 128), F32),
            pltpu.VMEM((nsec, chunks * per_sec, 128), F32),
            pltpu.VMEM((4,) + eigvecs.shape, F32),
            pltpu.VMEM((nblk // 4, per_sec, 128), F32),
            pltpu.VMEM((nblk // 4, per_sec, 128), F32),
            pltpu.VMEM(tile, F32),
            pltpu.VMEM(tile, F32),
            pltpu.VMEM((comps * elems * fields, 3 * pts), F32),
            pltpu.SemaphoreType.DMA((nsec,)),
            pltpu.SemaphoreType.DMA((nsec,)),
            pltpu.SemaphoreType.DMA((4,)),
            pltpu.SemaphoreType.DMA((4,)),
            pltpu.SemaphoreType.DMA((nblk // 4,)),
            pltpu.SemaphoreType.DMA((nblk // 4,)),
            pltpu.SemaphoreType.DMA((nblk,)),
            pltpu.SemaphoreType.DMA((nblk,)),
        ],
        compiler_params=pltpu.CompilerParams(
            collective_id=0, has_side_effects=True),
    )(velocity, *mats, geometry, mass, weights, snapshots, elem_map, eigvecs, mo)
    return out * factor


def solution(mesh):
    placed = (
        P(None, None, ("sec", "blk"), None),
        P(None, ("sec", "blk"), None),
        P(("sec", "blk"), None),
        P(None, None, ("sec", "blk"), None),
        P("blk", None),
        P(),
        P(("sec", "blk")),
    )
    return jax.shard_map(
        shards, mesh=mesh, in_specs=placed, out_specs=P("sec", "blk"), check_vma=False
    )
```
